512 devices in a mesh: halo: 8 (over x, core), leaf: 64 (over y, z).
Axes of the slice: x: 4, y: 8, z: 8, core: 2. Of those that a mesh axis runs over, the one named last changes fastest.
Arguments:
- start_modes: bfloat16 [64, 128, 32, 4, 128], P('leaf', None, 'halo'), may hold values from -6 to 6
- density: float32 [64, 32, 4, 128], P('leaf', 'halo'), may hold values from 0.5 to 4
- planes: int32 [64], P('leaf'), may hold values from 1 to 32, 1071 in all
- tree_order: int32 [64], replicated, may hold values from 0 to 63, each once
- iface_index: int32 [64, 2, 128], P('leaf', None, 'halo'), may hold values from 0 to 2047
- iface_stiff: float32 [64, 2, 128], P('leaf', None, 'halo'), may hold values from 0.5 to 2
- reduced_start: float32 [384, 128], replicated, may hold values from -6 to 6
Outputs:
- modes: float32 [64, 128, 32, 4, 128], P('leaf', None, 'halo')
- reduced: float32 [64, 128, 128], P('leaf')
The draws below stay inside these ranges and needn't reach their ends.
All inputs are finite; a program needn't handle non-finite values. No bound on the sum of `planes` on one device may be relied on, other than what follows from the above.
Results may differ from the reference program's by a relative error of at most 0.0003.
Values sent between devices are 32-bit elements; how exact they have to be, the bound alone decides.
No kernel may reach another device: no remote copies, remote signals or barrier semaphores. Data moves between devices by JAX's collectives and lax.ppermute only.
A program may use at most 64 MiB of HBM per device.

```python
import functools
import math
import jax
import jax.numpy as jnp
import numpy as np
from jax import lax

KEEP = 128
CX = 4
CY = 4
CZ = 128
ITERS = 2
RITERS = 2
LEVELS = 2
NXS = 32
CELLS = 16384
IFACE = 16
ORDER = 384
N_LEAF = 64


def place_ends(drawn, key, low, high):
    longest = drawn.shape.index(max(drawn.shape))
    spots = []
    for shift in (0, 1):
        where = [jax.random.randint(jax.random.fold_in(key, axis), (), 0, length) for axis, length in enumerate(drawn.shape)]
        where[longest] = (where[longest] + shift) % drawn.shape[longest]
        spots.append(tuple(where))
    return drawn.at[spots[0]].set(low).at[spots[1]].set(high)


def shard_levels(key, dims, split, least, largest):
    def one(axis_at, parts):
        steps = jax.random.uniform(jax.random.fold_in(jax.random.fold_in(key, 6), axis_at), (parts,), jnp.float32, least / len(split), largest / len(split))
        return jnp.repeat(jnp.exp(steps), dims[axis_at] // parts).reshape((-1,) + (1,) * (len(dims) - axis_at - 1))

    gain = one(*split[0])
    for cut in split[1:]:
        gain = gain * one(*cut)
    return gain


def profile(amount, total, reach, lean):
    portions = [(1 << 20) // math.isqrt(standing ** lean) + 1 for standing in range(2, amount + 1)]
    rest, counts = total - reach - (amount - 1), [1] * (amount - 1)
    while rest > 0:
        movable = [i for i in range(amount - 1) if counts[i] < reach]
        mass, remaining = sum([portions[i] for i in movable]), rest
        for i in movable:
            more = min(reach - counts[i], max(1, remaining * portions[i] // mass), rest)
            counts[i] = counts[i] + more
            rest = rest - more
    return np.array([reach] + counts)


def ragged_sizes(rng, amount, total, most, slope):
    if amount == 2:
        one = jax.random.randint(rng, (), max(1, total - most), min(most, total - 1) + 1)
        return jnp.stack([one, total - one])
    lengths = jnp.asarray(profile(amount, total, most, slope), jnp.int32)
    couples = (amount - 1) // 2
    source_of, taker = lengths[1:1 + 2 * couples:2], lengths[2:2 + 2 * couples:2]
    slack = jnp.minimum(source_of - 1, most - taker)
    moved = jax.random.randint(jax.random.fold_in(rng, 1), (couples,), 0, 1 << 20) % (slack + 1)
    lengths = lengths.at[1:1 + 2 * couples:2].set(source_of - moved).at[2:2 + 2 * couples:2].set(taker + moved)
    return lengths[jax.random.permutation(jax.random.fold_in(rng, 2), amount)]


def scatter_about(stream_key, shape, scale, limit, pieces=(), held_as=jnp.bfloat16):
    gain = shard_levels(stream_key, shape, pieces, -0.22, 0.18) if pieces else 1.0
    values = jax.random.normal(stream_key, shape, jnp.float32) * scale * gain
    return jnp.minimum(jnp.maximum(values, -limit), limit).astype(held_as)


def setup_inputs(seed: int = 0) -> dict:
    seeds = jax.random.split(jax.random.key(seed), 8)
    start_modes = scatter_about(seeds[0], (N_LEAF, KEEP, NXS, CY, CZ), 1.0, 6.0, ((0, 64), (2, 8)))
    density = jnp.clip(jnp.exp(math.log(4.0) - 2.0794415 * jax.random.uniform(seeds[1], (N_LEAF, NXS, CY, CZ), jnp.float32) ** shard_levels(seeds[1], (N_LEAF, NXS, CY, CZ), ((0, 64), (1, 8)), -0.2, 0.2)), 0.5, 4.0)
    planes = ragged_sizes(seeds[2], N_LEAF, (N_LEAF - 1) + NXS + (N_LEAF - 1) * (NXS - 1) // 2, NXS, 2).astype(jnp.int32)
    tree_order = jax.random.permutation(seeds[3], N_LEAF).astype(jnp.int32)
    iface_index = place_ends(jax.random.randint(seeds[4], (N_LEAF, LEVELS, KEEP), 0, CX * CY * CZ), jax.random.fold_in(seeds[4], 1), 0, (CX * CY * CZ) - 1).astype(jnp.int32)
    iface_stiff = jnp.clip(jnp.exp(math.log(2.0) - 1.3862944 * jax.random.uniform(seeds[5], (N_LEAF, LEVELS, KEEP), jnp.float32) ** shard_levels(seeds[5], (N_LEAF, LEVELS, KEEP), ((0, 64), (2, 8)), -0.2, 0.2)), 0.5, 2.0)
    reduced_start = scatter_about(seeds[6], (ORDER, KEEP), 1.0, 6.0, (), jnp.float32)
    return dict(start_modes=start_modes, density=density, planes=planes, tree_order=tree_order, iface_index=iface_index, iface_stiff=iface_stiff, reduced_start=reduced_start)


EXACT = lax.Precision.HIGHEST

def axis_smooth(values_in, axis_number):
    pads = [(1, 1) if position == axis_number else (0, 0) for position in range(values_in.ndim)]
    padded = jnp.pad(values_in, pads)
    extent = values_in.shape[axis_number]
    return 0.5 * lax.slice_in_dim(padded, 0, extent, axis=axis_number) + lax.slice_in_dim(padded, 1, extent + 1, axis=axis_number) + 0.5 * lax.slice_in_dim(padded, 2, extent + 2, axis=axis_number)

def operator_apply(vectors, density_cells, plane_mask):
    masked = vectors * plane_mask
    stacked = jnp.stack([masked, masked * density_cells])
    summed = axis_smooth(stacked, 2)
    summed = axis_smooth(summed, 3)
    summed = axis_smooth(summed, 4)
    return plane_mask * (density_cells * summed[0] + summed[1]) / 16.0

def reduce_solve(own_reduced, other_reduced, own_rows, other_rows, stiff_all, own_first, start_block, coupling_scale):
    first_reduced = jnp.where(own_first, own_reduced, other_reduced)
    second_reduced = jnp.where(own_first, other_reduced, own_reduced)
    first_rows = coupling_scale * jnp.where(own_first, own_rows, other_rows)
    second_rows = coupling_scale * jnp.where(own_first, other_rows, own_rows)
    zero_block = jnp.zeros_like(first_reduced)
    matrix = jnp.block([[first_reduced, zero_block, first_rows.T], [zero_block, second_reduced, second_rows.T], [first_rows, second_rows, jnp.diag(stiff_all)]])
    coeffs = start_block
    for inner_step in range(RITERS):
        product = jnp.dot(matrix, coeffs, precision=EXACT)
        gram_small = jnp.dot(product.T, product, precision=EXACT)
        lower_factor = jnp.linalg.cholesky(gram_small)
        coeffs = jax.scipy.linalg.solve_triangular(lower_factor, product.T, lower=True).T
    reduced_next = jnp.dot(coeffs.T, jnp.dot(matrix, coeffs, precision=EXACT), precision=EXACT)
    return (coeffs, reduced_next)

def subspace_phase(inputs):
    start_one, density_one, planes_one = inputs
    plane_mask = (jnp.arange(NXS, dtype=jnp.int32) < planes_one).astype(jnp.float32)[:, None, None]
    vectors = start_one.astype(jnp.float32)
    for iteration in range(ITERS - 1):
        vectors = operator_apply(vectors, density_one, plane_mask)
    image_rows = operator_apply(vectors, density_one, plane_mask).reshape(KEEP, CELLS)
    gram_total = jnp.einsum('kp,jp->kj', image_rows, image_rows, precision=EXACT)
    lower_factor = jnp.linalg.cholesky(gram_total)
    basis_rows = jax.scipy.linalg.solve_triangular(lower_factor, image_rows, lower=True)
    applied = operator_apply(basis_rows.reshape(KEEP, NXS, CY, CZ), density_one, plane_mask).reshape(KEEP, CELLS)
    reduced_one = jnp.einsum('kp,jp->kj', basis_rows, applied, precision=EXACT)
    return (basis_rows, reduced_one)

def reference(start_modes, density, planes, tree_order, iface_index, iface_stiff, reduced_start):
    basis_all, reduced_all = lax.map(subspace_phase, (start_modes, density, planes))
    leaf_ids = jnp.arange(N_LEAF, dtype=jnp.int32)
    coupling_scale = 0.5 * math.sqrt(CELLS / KEEP)
    for level_index in range(LEVELS):
        group_step = 2 ** level_index
        blocks = tree_order // group_step
        other_blocks = jnp.bitwise_xor(blocks, 1)
        own_mask = blocks[None, :] == blocks[:, None]
        same_mask = own_mask & (leaf_ids[None, :] != leaf_ids[:, None])
        other_mask = blocks[None, :] == other_blocks[:, None]
        rep_mask = tree_order[None, :] == (other_blocks * group_step)[:, None]
        own_least = lax.optimization_barrier(jnp.min(jnp.where(own_mask, leaf_ids[None, :], N_LEAF), axis=1))
        other_least = lax.optimization_barrier(jnp.min(jnp.where(other_mask, leaf_ids[None, :], N_LEAF), axis=1))
        own_first = own_least < other_least
        cell_index = (jnp.arange(KEEP, dtype=jnp.int32) // IFACE * (CX * CY * CZ))[None, :] + iface_index[:, level_index, :]
        rows_all = jax.vmap(lambda basis_one, index_one: jnp.take(basis_one, index_one, axis=1).T)(basis_all, cell_index)
        same_weight = same_mask.astype(jnp.float32)
        other_weight = other_mask.astype(jnp.float32)
        rep_weight = rep_mask.astype(jnp.float32)
        own_rows = rows_all + jnp.einsum('st,tjk->sjk', same_weight, rows_all, precision=EXACT)
        other_rows = jnp.einsum('st,tjk->sjk', other_weight, rows_all, precision=EXACT)
        stiffness = iface_stiff[:, level_index, :]
        stiff_all = stiffness + jnp.einsum('st,tj->sj', same_weight + other_weight, stiffness, precision=EXACT)
        other_reduced = jnp.einsum('st,tjk->sjk', rep_weight, reduced_all, precision=EXACT)
        solver = functools.partial(reduce_solve, start_block=reduced_start, coupling_scale=coupling_scale)
        coeffs_all, reduced_next = jax.vmap(solver)(reduced_all, other_reduced, own_rows, other_rows, stiff_all, own_first)
        weight_factor = 1.0 / math.sqrt(2 ** (level_index + 1))

        def update_basis(inputs):
            basis_one, coeffs_one, index_one, first_one = inputs
            own_coeffs = jnp.where(first_one, coeffs_one[:KEEP], coeffs_one[KEEP:2 * KEEP])
            iface_coeffs = coeffs_one[2 * KEEP:]
            spread = jnp.zeros((KEEP, CELLS), jnp.float32).at[:, index_one].add(weight_factor * iface_coeffs.T)
            return jnp.einsum('kj,kp->jp', own_coeffs, basis_one, precision=EXACT) + spread
        basis_all = lax.map(update_basis, (basis_all, coeffs_all, cell_index, own_first))
        reduced_all = reduced_next
    modes = (math.sqrt(CELLS) * basis_all).reshape(N_LEAF, KEEP, NXS, CY, CZ)
    return (modes, reduced_all)
```

```python
import math

import jax
import jax.numpy as jnp
from jax import lax
from jax.experimental import pallas as pl
from jax.experimental.pallas import tpu as pltpu
from jax.sharding import PartitionSpec as P

F32 = jnp.float32
HI = lax.Precision.HIGHEST
NV = 128
NC = 2048
SQ = 8
ROWS = 56
AG = 3 * ROWS + 40
VM = pl.BlockSpec(memory_space=pltpu.VMEM)
SM = pl.BlockSpec(memory_space=pltpu.SMEM)


def dot_nt(a, b):
    return lax.dot_general(a, b, (((1,), (1,)), ((), ())), precision=HI, preferred_element_type=F32)


def dot_nn(a, b):
    return lax.dot_general(a, b, (((1,), (0,)), ((), ())), precision=HI, preferred_element_type=F32)


def dot_tn(a, b):
    return lax.dot_general(a, b, (((0,), (0,)), ((), ())), precision=HI, preferred_element_type=F32)


def iota(shape, dim):
    return lax.broadcasted_iota(jnp.int32, shape, dim)


def shape(*dims):
    return jax.ShapeDtypeStruct(dims, F32)


def chol_inv(mats):
    count = len(mats)
    sh = (count, 8, NV)
    lane, sub = iota(sh, 2), iota(sh, 1)

    def over_lanes(x, c):
        return jnp.broadcast_to(x[:, :, c : c + 1], sh)

    def over_subs(x, r):
        return jnp.broadcast_to(x[:, r : r + 1, :], sh)

    rows = [jnp.stack([m[8 * i : 8 * i + 8, :] for m in mats]) for i in range(16)]
    for s in range(16):
        p = rows[s]
        cols = [over_lanes(p, 8 * s + j) for j in range(8)]
        scaled, scales, upper = [], [], {}
        for k in range(8):
            rs = lax.rsqrt(over_subs(cols[k], k))
            at = lane == 8 * s + k
            r = jnp.where(at, rs, over_subs(p, k) * rs)
            scaled.append(r)
            scales.append(rs)
            if k < 7:
                low = cols[k] * rs
                p = jnp.where(sub > k, jnp.where(at, 0.0, p) - low * r, p)
                for j in range(k + 1, 8):
                    upper[k, j] = over_subs(cols[j], k) * rs
                    cols[j] = cols[j] - low * upper[k, j]
        out = scaled[7]
        for k in range(7):
            out = jnp.where(sub == k, scaled[k], out)
        rows[s] = jnp.where(lane > 8 * s + sub, 0.0, out)
        inside = (lane >= 8 * s) & (lane < 8 * s + 8)
        kept = [jnp.where(inside & (lane > 8 * s + k), 0.0, scaled[k]) for k in range(8)]
        for a in range(s + 1, 16):
            q = rows[a]
            cols = [over_lanes(q, 8 * s + j) for j in range(8)]
            q = jnp.where(inside, 0.0, q)
            for k in range(8):
                low = cols[k] * scales[k]
                q = q - low * kept[k]
                for j in range(k + 1, 8):
                    cols[j] = cols[j] - low * upper[k, j]
            rows[a] = q
    return [jnp.concatenate([rows[i][b] for i in range(16)], axis=0) for b in range(count)]


def prep_kernel(planes, v, rho, left, right, wide):
    h = lax.axis_index("halo")
    wide[...] = v[...].astype(F32)
    for k in range(16):
        part = wide[pl.ds(k, NV, stride=16), :]
        part = jnp.where(h * 4 + k // 4 < planes[0], part, 0.0)
        if k < 12:
            left[k * NV : (k + 1) * NV, :] = part
        if k >= 4:
            right[(k - 4) * NV : (k - 3) * NV, :] = part
    left[12 * NV :, :] = rho[...]
    right[12 * NV : 12 * NV + 12, :] = rho[4:, :]
    right[12 * NV + 12 :, :] = rho[:4, :]


def smooth_first(cells):
    pairs = [[a + b for a, b in zip(lo, hi)] for lo, hi in zip(cells[:-1], cells[1:])]
    return [[a + b for a, b in zip(lo, hi)] for lo, hi in zip(pairs[:-1], pairs[1:])]


def smooth_second(row):
    pairs = [a + b for a, b in zip(row[:-1], row[1:])]
    return [a + b for a, b in zip([row[0]] + pairs, pairs + [row[-1]])]


def front_kernel(planes, index, left, right, from_left, from_right, w_out, full_out, wg_out, rho_s, both, hot):
    h = lax.axis_index("halo")
    lane = iota((8, NV), 1)
    half_lo = jnp.where(lane == 0, 0.0, 0.5).astype(F32)
    half_hi = jnp.where(lane == NV - 1, 0.0, 0.5).astype(F32)
    on = [jnp.where((h * 4 + q >= 0) & (h * 4 + q < planes[0]), 1.0 / 64, 0.0) for q in range(-3, 7)]

    def place(q):
        if q < 0:
            return from_left, q + 3
        if q < 3:
            return left, q
        if q == 3:
            return right, 2
        return from_right, q - 4

    for q in range(-3, 7):
        ref, p = place(q)
        for c in range(4):
            row = 12 * NV + 4 * p + c
            rho_s[q + 3, c] = jnp.broadcast_to(ref[row : row + 1, :], (8, NV))

    def smooth_third(x):
        return x + half_lo * pltpu.roll(x, 1, 1) + half_hi * pltpu.roll(x, NV - 1, 1)

    def apply(cells, lo):
        dense = [[rho_s[lo + i, c] * x for c, x in enumerate(row)] for i, row in enumerate(cells)]
        plain, dense = smooth_first(cells), smooth_first(dense)
        out = []
        for i, (pr, dr) in enumerate(zip(plain, dense)):
            pr, dr = smooth_second(pr), smooth_second(dr)
            q = lo + 1 + i
            out.append(
                [(rho_s[q, c] * smooth_third(x) + smooth_third(y)) * on[q] for c, (x, y) in enumerate(zip(pr, dr))]
            )
        return out

    def group(g, carry):
        cells = []
        for q in range(-3, 7):
            ref, p = place(q)
            cells.append([ref[pl.ds(pl.multiple_of((4 * p + c) * NV + g * 8, 8), 8), :] for c in range(4)])
        cells = apply(apply(cells, 0), 1)
        rows = pl.ds(pl.multiple_of(g * 8, 8), 8)
        for p in range(4):
            for c in range(4):
                k = 4 * p + c
                both[rows, k * NV : (k + 1) * NV] = cells[p + 1][c]
        cells = apply(cells, 2)
        rows = pl.ds(pl.multiple_of(NV + g * 8, 8), 8)
        for p in range(4):
            for c in range(4):
                k = 4 * p + c
                both[rows, k * NV : (k + 1) * NV] = cells[p][c]
        return carry

    lax.fori_loop(0, NV // 8, group, 0)
    fill_hot(index, hot, F32)
    w = both[:NV, :]
    w_out[...] = w
    gram = dot_nt(w, both[...])
    wg_out[...] = dot_nt(hot[...], w)
    row, col = iota((NV, NV), 0), iota((NV, NV), 1)
    s, c = gram[:, :NV], gram[:, NV:]
    packed = jnp.where(row >= col, s, c)
    diag = jnp.sum(jnp.where(row == col, c, 0.0), axis=0, keepdims=True)
    for peer in range(8):
        full_out[peer, :NV, :] = packed
        full_out[peer, NV:, :] = jnp.broadcast_to(diag, (8, NV))


def fill_hot(index, hot, dtype):
    for part in range(4):
        sub = iota((8, NV), 0)
        col = jnp.zeros((8, NV), jnp.int32)
        for j in range(8):
            col = jnp.where(sub == j, index[0, part // 2, (part % 2) * 8 + j], col)
        lane = iota((8, NV), 1)
        for k in range(16):
            hot[part * 8 : part * 8 + 8, k * NV : (k + 1) * NV] = jnp.where(col == lane + k * NV, 1.0, 0.0).astype(dtype)


def own_kernel(full, wg, stiff, index, li_out, k_out, message, small):
    h = lax.axis_index("halo")
    total = jnp.sum(full[...], axis=0)
    packed, diag = total[:NV, :], total[NV : NV + 1, :]
    row, col = iota((NV, NV), 0), iota((NV, NV), 1)
    mirror = packed.T
    s = jnp.where(row >= col, packed, mirror)
    c = jnp.where(row < col, packed, jnp.where(row > col, mirror, diag))
    (li,) = chol_inv([s])
    k = dot_nt(dot_nn(li, c), li)
    li_out[...] = li
    k_out[...] = k
    rows = dot_nt(wg[...], li)
    small[...] = jnp.zeros((8, NV), F32)
    small[0:2, 0:16] = stiff[0]
    small[2:4, 0:16] = (index[0] + h * NC).astype(F32)
    spread = pltpu.roll(small[...], h * 16, 1)
    mine = k_out[pl.ds(pl.multiple_of(h * 16, 16), 16), :]
    for peer in range(SQ):
        message[peer, :16, :] = mine
        message[peer, 16:48, :] = rows
        message[peer, 48:, :] = spread


def invert(order, inverse):
    for t in range(SQ * SQ):
        inverse[order[t]] = t


def select_kernel(order, got, out, inverse):
    leaf = lax.axis_index("leaf")
    y, z = leaf // SQ, leaf % SQ
    invert(order, inverse)
    for to in range(SQ):
        position = order[to * SQ + z]
        for role in range(1, 4):
            source = inverse[position ^ role]
            part = got[source % SQ]
            out[to, (role - 1) * ROWS : role * ROWS, :] = jnp.where(source // SQ == y, part, 0.0)


def collect_kernel(got, message, out):
    total = jnp.sum(got[...], axis=0)
    own = message[0, 16:, :]
    for peer in range(4):
        out[peer, : 3 * ROWS, :] = total
        out[peer, 3 * ROWS :, :] = own


def solve_kernel(
    order, index, mine, other, k_own, li, w, start, modes_out, reduced_out, inverse, kmat, rmat, big, z_s, hot
):
    h, leaf = lax.axis_index("halo"), lax.axis_index("leaf")
    odd = h % 2
    invert(order, inverse)
    position = order[leaf]
    ids = [leaf] + [inverse[position ^ role] for role in range(1, 4)]
    scale = 0.5 * math.sqrt(NC * 8 / NV)

    def piece(halo, lo, hi):
        a, b = mine[halo // 2, lo:hi, :], other[halo // 2, lo:hi, :]
        return jnp.where(odd == halo % 2, a, b)

    small = []
    kmat[0] = k_own[...]
    for role in range(4):
        base = 3 * ROWS - 16 if role == 0 else (role - 1) * ROWS
        for halo in range(8):
            at = slice(16 * halo, 16 * halo + 16)
            if role:
                kmat[role, at, :] = piece(halo, base, base + 16)
            rmat[0, role, at, :] = piece(halo, base + 16, base + 32)
            rmat[1, role, at, :] = piece(halo, base + 32, base + 48)
        tiles = [piece(halo, base + 48, base + 56) for halo in range(8)]
        small.append(sum(tiles[1:], tiles[0]))

    row, col = iota((NV, NV), 0), iota((NV, NV), 1)
    eye = row == col

    def meet(slot, first, ka, ra, kb, rb, stiff):
        zero = jnp.zeros((NV, NV), F32)
        ra, rb = scale * ra, scale * rb
        r1, r2 = jnp.where(first, ra, rb), jnp.where(first, rb, ra)
        big[slot, :NV, :NV] = jnp.where(first, ka, kb)
        big[slot, :NV, NV : 2 * NV] = zero
        big[slot, :NV, 2 * NV :] = r1.T
        big[slot, NV : 2 * NV, :NV] = zero
        big[slot, NV : 2 * NV, NV : 2 * NV] = jnp.where(first, kb, ka)
        big[slot, NV : 2 * NV, 2 * NV :] = r2.T
        big[slot, 2 * NV :, :NV] = r1
        big[slot, 2 * NV :, NV : 2 * NV] = r2
        big[slot, 2 * NV :, 2 * NV :] = jnp.where(eye, stiff, 0.0)

    def reduce(slots):
        ys = [dot_nn(big[i], dot_nn(big[i], start[...])) for i in slots]
        ps = chol_inv([dot_tn(y, y) for y in ys])
        images = [dot_tn(y, dot_nn(big[i], y)) for i, y in zip(slots, ys)]
        return [dot_nt(y, p) for y, p in zip(ys, ps)], [dot_nt(dot_nn(p, im), p) for p, im in zip(ps, images)]

    firsts = [ids[0] < ids[1], ids[2] < ids[3]]
    for pair in range(2):
        a, b = 2 * pair, 2 * pair + 1
        meet(pair, firsts[pair], kmat[a], rmat[0, a], kmat[b], rmat[0, b], small[a][0:1] + small[b][0:1])
    zs, ks = reduce([0, 1])
    joint = []
    for pair in range(2):
        z = zs[pair]
        lo, hi, zi = z[:NV], z[NV : 2 * NV], z[2 * NV :]
        za, zb = jnp.where(firsts[pair], lo, hi), jnp.where(firsts[pair], hi, lo)
        match = jnp.zeros((NV, NV), F32)
        for role in (2 * pair, 2 * pair + 1):
            up = jnp.sum(jnp.where(eye, small[role][3:4], 0.0), axis=1, keepdims=True)
            match = match + jnp.where(up == small[role][2:3], 1.0, 0.0)
        joint.append(
            dot_nn(rmat[1, 2 * pair], za) + dot_nn(rmat[1, 2 * pair + 1], zb) + math.sqrt(0.5) * dot_nn(match, zi)
        )
        if pair == 0:
            z_s[:NV, :] = za
            z_s[NV:, :] = zi
    first = jnp.minimum(ids[0], ids[1]) < jnp.minimum(ids[2], ids[3])
    stiff = small[0][1:2] + small[1][1:2] + small[2][1:2] + small[3][1:2]
    meet(0, first, ks[0], joint[0], ks[1], joint[1], stiff)
    (z1,), (k1,) = reduce([0])
    reduced_out[...] = k1
    top = jnp.where(first, z1[:NV], z1[NV : 2 * NV])
    at = pl.ds(pl.multiple_of(NV + h * 16, 16), 16)
    low_part = z_s[at, :]
    z_low = z_s[:NV, :]
    z_s[NV:, :] = z1[2 * NV :]
    top_part = z_s[at, :]
    final = math.sqrt(NC * 8)
    mixed = final * dot_tn(top, dot_tn(z_low, li[...]))
    spread = jnp.concatenate([math.sqrt(0.5) * final * dot_nn(low_part, top), 0.5 * final * top_part], axis=0)
    fill_hot(index, hot, F32)
    for k in range(16):
        at = slice(k * NV, (k + 1) * NV)
        part = dot_nn(mixed, w[:, at]) + dot_tn(spread, hot[:, at])
        modes_out[pl.ds(k, NV, stride=16), :] = part


def per_device(start_modes, density, planes, tree_order, iface_index, iface_stiff, reduced_start):
    row_groups = [[y * SQ + z for z in range(SQ)] for y in range(SQ)]
    col_groups = [[y * SQ + z for y in range(SQ)] for z in range(SQ)]
    chips = [[0, 2, 4, 6], [1, 3, 5, 7]]
    edge = 12 * NV + 16
    left, right = pl.pallas_call(
        prep_kernel,
        out_shape=(shape(edge, NV), shape(edge, NV)),
        in_specs=[SM, VM, VM],
        out_specs=(VM, VM),
        scratch_shapes=[pltpu.VMEM((NC, NV), F32)],
        name="prep",
    )(planes, start_modes.reshape(NC, NV), density.reshape(16, NV))
    from_left = lax.ppermute(right, "halo", [(i, i + 1) for i in range(7)])
    from_right = lax.ppermute(left, "halo", [(i + 1, i) for i in range(7)])
    w, full, wg = pl.pallas_call(
        front_kernel,
        out_shape=(shape(NV, NC), shape(8, NV + 8, NV), shape(32, NV)),
        in_specs=[SM, SM, VM, VM, VM, VM],
        out_specs=(VM, VM, VM),
        scratch_shapes=[
            pltpu.VMEM((10, 4, 8, NV), F32),
            pltpu.VMEM((2 * NV, NC), F32),
            pltpu.VMEM((32, NC), F32),
        ],
        name="front",
    )(planes, iface_index, left, right, from_left, from_right)
    full = lax.all_to_all(full, "halo", 0, 0, tiled=True)
    li, k_own, message = pl.pallas_call(
        own_kernel,
        out_shape=(shape(NV, NV), shape(NV, NV), shape(SQ, ROWS, NV)),
        in_specs=[VM, VM, VM, VM],
        out_specs=(VM, VM, VM),
        scratch_shapes=[pltpu.VMEM((8, NV), F32)],
        name="own",
    )(full, wg, iface_stiff, iface_index)
    along = lax.all_to_all(message, "leaf", 0, 0, tiled=True, axis_index_groups=row_groups)
    chosen = pl.pallas_call(
        select_kernel,
        out_shape=shape(SQ, 3 * ROWS, NV),
        in_specs=[SM, VM],
        out_specs=VM,
        scratch_shapes=[pltpu.SMEM((SQ * SQ,), jnp.int32)],
        name="select",
    )(tree_order, along)
    across = lax.all_to_all(chosen, "leaf", 0, 0, tiled=True, axis_index_groups=col_groups)
    gathered = pl.pallas_call(
        collect_kernel,
        out_shape=shape(4, AG, NV),
        in_specs=[VM, VM],
        out_specs=VM,
        name="collect",
    )(across, message)
    mine = lax.all_to_all(gathered, "halo", 0, 0, tiled=True, axis_index_groups=chips)
    other = lax.ppermute(mine, "halo", [(i, i ^ 1) for i in range(8)])
    modes, reduced = pl.pallas_call(
        solve_kernel,
        out_shape=(shape(NC, NV), shape(NV, NV)),
        in_specs=[SM, SM, VM, VM, VM, VM, VM, VM],
        out_specs=(VM, VM),
        scratch_shapes=[
            pltpu.SMEM((SQ * SQ,), jnp.int32),
            pltpu.VMEM((4, NV, NV), F32),
            pltpu.VMEM((2, 4, NV, NV), F32),
            pltpu.VMEM((2, 3 * NV, 3 * NV), F32),
            pltpu.VMEM((2 * NV, NV), F32),
            pltpu.VMEM((32, NC), F32),
        ],
        name="solve",
    )(tree_order, iface_index, mine, other, k_own, li, w, reduced_start)
    return modes.reshape(1, NV, 4, 4, NV), reduced[None]


def solution(mesh):
    return jax.shard_map(
        per_device,
        mesh=mesh,
        in_specs=(
            P("leaf", None, "halo", None, None),
            P("leaf", "halo", None, None),
            P("leaf"),
            P(),
            P("leaf", None, "halo"),
            P("leaf", None, "halo"),
            P(),
        ),
        out_specs=(P("leaf", None, "halo", None, None), P("leaf", None, None)),
        check_vma=False,
    )
```

```python
import math

import jax
import jax.numpy as jnp
from jax import lax
from jax.experimental import pallas as pl
from jax.experimental.pallas import tpu as pltpu
from jax.sharding import PartitionSpec as P

F32 = jnp.float32
HI = lax.Precision.HIGHEST
NV = 128
NC = 2048
SQ = 8
ROWS = 48
AG = 3 * ROWS + 40
VM = pl.BlockSpec(memory_space=pltpu.VMEM)
SM = pl.BlockSpec(memory_space=pltpu.SMEM)


def dot_nt(a, b):
    return lax.dot_general(a, b, (((1,), (1,)), ((), ())), precision=HI, preferred_element_type=F32)


def dot_nn(a, b):
    return lax.dot_general(a, b, (((1,), (0,)), ((), ())), precision=HI, preferred_element_type=F32)


def dot_tn(a, b):
    return lax.dot_general(a, b, (((0,), (0,)), ((), ())), precision=HI, preferred_element_type=F32)


def iota(shape, dim):
    return lax.broadcasted_iota(jnp.int32, shape, dim)


def grant(mib):
    return pltpu.CompilerParams(vmem_limit_bytes=mib << 20)


def shape(*dims):
    return jax.ShapeDtypeStruct(dims, F32)


def chol_inv(mats):
    count = len(mats)
    sh = (count, 8, NV)
    lane, sub = iota(sh, 2), iota(sh, 1)

    def over_lanes(x, c):
        return jnp.broadcast_to(x[:, :, c : c + 1], sh)

    def over_subs(x, r):
        return jnp.broadcast_to(x[:, r : r + 1, :], sh)

    rows = [jnp.stack([m[8 * i : 8 * i + 8, :] for m in mats]) for i in range(16)]
    for s in range(16):
        p = rows[s]
        cols = [over_lanes(p, 8 * s + j) for j in range(8)]
        scaled, scales, upper = [], [], {}
        for k in range(8):
            rs = lax.rsqrt(over_subs(cols[k], k))
            at = lane == 8 * s + k
            r = jnp.where(at, rs, over_subs(p, k) * rs)
            scaled.append(r)
            scales.append(rs)
            if k < 7:
                low = cols[k] * rs
                p = jnp.where(sub > k, jnp.where(at, 0.0, p) - low * r, p)
                for j in range(k + 1, 8):
                    upper[k, j] = over_subs(cols[j], k) * rs
                    cols[j] = cols[j] - low * upper[k, j]
        out = scaled[7]
        for k in range(7):
            out = jnp.where(sub == k, scaled[k], out)
        rows[s] = jnp.where(lane > 8 * s + sub, 0.0, out)
        inside = (lane >= 8 * s) & (lane < 8 * s + 8)
        kept = [jnp.where(inside & (lane > 8 * s + k), 0.0, scaled[k]) for k in range(8)]
        for a in range(s + 1, 16):
            q = rows[a]
            cols = [over_lanes(q, 8 * s + j) for j in range(8)]
            q = jnp.where(inside, 0.0, q)
            for k in range(8):
                low = cols[k] * scales[k]
                q = q - low * kept[k]
                for j in range(k + 1, 8):
                    cols[j] = cols[j] - low * upper[k, j]
            rows[a] = q
    return [jnp.concatenate([rows[i][b] for i in range(16)], axis=0) for b in range(count)]


def prep_kernel(planes, v, rho, left, right, wide):
    h = lax.axis_index("halo")
    wide[...] = v[...].astype(F32)
    for k in range(16):
        part = wide[pl.ds(k, NV, stride=16), :]
        part = jnp.where(h * 4 + k // 4 < planes[0], part, 0.0)
        if k < 12:
            left[k * NV : (k + 1) * NV, :] = part
        if k >= 4:
            right[(k - 4) * NV : (k - 3) * NV, :] = part
    left[12 * NV :, :] = rho[...]
    right[12 * NV : 12 * NV + 12, :] = rho[4:, :]
    right[12 * NV + 12 :, :] = rho[:4, :]


def smooth_first(cells):
    pairs = [[a + b for a, b in zip(lo, hi)] for lo, hi in zip(cells[:-1], cells[1:])]
    return [[a + b for a, b in zip(lo, hi)] for lo, hi in zip(pairs[:-1], pairs[1:])]


def smooth_second(row):
    pairs = [a + b for a, b in zip(row[:-1], row[1:])]
    return [a + b for a, b in zip([row[0]] + pairs, pairs + [row[-1]])]


def front_kernel(planes, index, left, right, from_left, from_right, w_out, full_out, wg_out, rho_s, both, hot):
    h = lax.axis_index("halo")
    lane = iota((8, NV), 1)
    half_lo = jnp.where(lane == 0, 0.0, 0.5).astype(F32)
    half_hi = jnp.where(lane == NV - 1, 0.0, 0.5).astype(F32)
    on = [jnp.where((h * 4 + q >= 0) & (h * 4 + q < planes[0]), 1.0 / 64, 0.0) for q in range(-3, 7)]

    def place(q):
        if q < 0:
            return from_left, q + 3
        if q < 3:
            return left, q
        if q == 3:
            return right, 2
        return from_right, q - 4

    for q in range(-3, 7):
        ref, p = place(q)
        for c in range(4):
            row = 12 * NV + 4 * p + c
            rho_s[q + 3, c] = jnp.broadcast_to(ref[row : row + 1, :], (8, NV))

    def smooth_third(x):
        return x + half_lo * pltpu.roll(x, 1, 1) + half_hi * pltpu.roll(x, NV - 1, 1)

    def apply(cells, lo):
        dense = [[rho_s[lo + i, c] * x for c, x in enumerate(row)] for i, row in enumerate(cells)]
        plain, dense = smooth_first(cells), smooth_first(dense)
        out = []
        for i, (pr, dr) in enumerate(zip(plain, dense)):
            pr, dr = smooth_second(pr), smooth_second(dr)
            q = lo + 1 + i
            out.append(
                [(rho_s[q, c] * smooth_third(x) + smooth_third(y)) * on[q] for c, (x, y) in enumerate(zip(pr, dr))]
            )
        return out

    def group(g, carry):
        cells = []
        for q in range(-3, 7):
            ref, p = place(q)
            cells.append([ref[pl.ds(pl.multiple_of((4 * p + c) * NV + g * 8, 8), 8), :] for c in range(4)])
        cells = apply(apply(cells, 0), 1)
        rows = pl.ds(pl.multiple_of(g * 8, 8), 8)
        for p in range(4):
            for c in range(4):
                k = 4 * p + c
                both[rows, k * NV : (k + 1) * NV] = cells[p + 1][c]
        cells = apply(cells, 2)
        rows = pl.ds(pl.multiple_of(NV + g * 8, 8), 8)
        for p in range(4):
            for c in range(4):
                k = 4 * p + c
                both[rows, k * NV : (k + 1) * NV] = cells[p][c]
        return carry

    lax.fori_loop(0, NV // 8, group, 0)
    fill_hot(index, hot, F32)
    w = both[:NV, :]
    w_out[...] = w
    gram = dot_nt(w, both[...])
    wg_out[...] = dot_nt(hot[...], w)
    row, col = iota((NV, NV), 0), iota((NV, NV), 1)
    s, c = gram[:, :NV], gram[:, NV:]
    packed = jnp.where(row >= col, s, c)
    diag = jnp.sum(jnp.where(row == col, c, 0.0), axis=0, keepdims=True)
    for peer in range(8):
        full_out[peer, :NV, :] = packed
        full_out[peer, NV:, :] = jnp.broadcast_to(diag, (8, NV))


def fill_hot(index, hot, dtype):
    for part in range(4):
        sub = iota((8, NV), 0)
        col = jnp.zeros((8, NV), jnp.int32)
        for j in range(8):
            col = jnp.where(sub == j, index[0, part // 2, (part % 2) * 8 + j], col)
        lane = iota((8, NV), 1)
        for k in range(16):
            hot[part * 8 : part * 8 + 8, k * NV : (k + 1) * NV] = jnp.where(col == lane + k * NV, 1.0, 0.0).astype(dtype)


def own_kernel(full, wg, stiff, index, li_out, k_out, message, small):
    h = lax.axis_index("halo")
    total = jnp.sum(full[...], axis=0)
    packed, diag = total[:NV, :], total[NV : NV + 1, :]
    row, col = iota((NV, NV), 0), iota((NV, NV), 1)
    mirror = packed.T
    s = jnp.where(row >= col, packed, mirror)
    c = jnp.where(row < col, packed, jnp.where(row > col, mirror, diag))
    (li,) = chol_inv([s])
    k = dot_nt(dot_nn(li, c), li)
    li_out[...] = li
    k_out[...] = k
    rows = dot_nt(wg[...], li)
    small[...] = jnp.zeros((8, NV), F32)
    small[0:2, 0:16] = stiff[0]
    small[2:4, 0:16] = (index[0] + h * NC).astype(F32)
    lane, sub = iota((8, NV), 1), iota((8, NV), 0)
    tile = small[...]
    tile = jnp.where(sub < 4, tile, pltpu.roll(pltpu.roll(tile, NV - 8, 1), 4, 0))
    tile = pltpu.roll(tile, h * 16, 1)
    upper = k_out[pl.ds(pl.multiple_of(h * 16, 16), 8), :]
    lower = k_out[pl.ds(pl.multiple_of(h * 16 + 8, 8), 8), :]
    lower = jnp.where((lane >= h * 16) & (lane < h * 16 + 8), tile, lower)
    for peer in range(SQ):
        message[peer, :8, :] = upper
        message[peer, 8:16, :] = lower
        message[peer, 16:, :] = rows


def invert(order, inverse):
    for t in range(SQ * SQ):
        inverse[order[t]] = t


def select_kernel(order, got, out, inverse):
    leaf = lax.axis_index("leaf")
    y, z = leaf // SQ, leaf % SQ
    invert(order, inverse)
    for to in range(SQ):
        position = order[to * SQ + z]
        for role in range(1, 4):
            source = inverse[position ^ role]
            @pl.when(source // SQ == y)
            def _(to=to, role=role, source=source):
                out[to, (role - 1) * ROWS : role * ROWS, :] = got[source % SQ]


def collect_kernel(order, got, message, out, inverse):
    leaf = lax.axis_index("leaf")
    invert(order, inverse)
    position = order[leaf]
    parts = [got[inverse[position ^ r] // SQ, (r - 1) * ROWS : r * ROWS, :] for r in range(1, 4)]
    own = message[0, 8:, :]
    for peer in range(4):
        for r in range(3):
            out[peer, r * ROWS : (r + 1) * ROWS, :] = parts[r]
        out[peer, 3 * ROWS :, :] = own


def solve_kernel(
    order, index, mine, other, k_own, li, w, start, modes_out, reduced_out, inverse, kmat, rmat, big, z_s, hot
):
    h, leaf = lax.axis_index("halo"), lax.axis_index("leaf")
    odd = h % 2
    invert(order, inverse)
    position = order[leaf]
    ids = [leaf] + [inverse[position ^ role] for role in range(1, 4)]
    scale = 0.5 * math.sqrt(NC * 8 / NV)

    def piece(halo, lo, hi):
        a, b = mine[halo // 2, lo:hi, :], other[halo // 2, lo:hi, :]
        return jnp.where(odd == halo % 2, a, b)

    row, col = iota((NV, NV), 0), iota((NV, NV), 1)
    eye = row == col
    lane = iota((8, NV), 1)
    small = []
    kmat[0] = k_own[...]
    for role in range(4):
        base = 3 * ROWS - 8 if role == 0 else (role - 1) * ROWS
        tile = jnp.zeros((8, NV), F32)
        for halo in range(8):
            at = slice(16 * halo, 16 * halo + 16)
            lower = piece(halo, base + 8, base + 16)
            if role:
                kmat[role, 16 * halo : 16 * halo + 8, :] = piece(halo, base, base + 8)
                kmat[role, 16 * halo + 8 : 16 * halo + 16, :] = lower
            rmat[0, role, at, :] = piece(halo, base + 16, base + 32)
            rmat[1, role, at, :] = piece(halo, base + 32, base + 48)
            tile = jnp.where((lane >= 16 * halo) & (lane < 16 * halo + 8), lower, tile)
        small.append(tile + pltpu.roll(pltpu.roll(tile, 8, 1), 4, 0))
        if role:
            raw = kmat[role]
            kmat[role] = jnp.where(row <= col, raw, raw.T)

    def meet(slot, first, ka, ra, kb, rb, stiff):
        zero = jnp.zeros((NV, NV), F32)
        ra, rb = scale * ra, scale * rb
        r1, r2 = jnp.where(first, ra, rb), jnp.where(first, rb, ra)
        big[slot, :NV, :NV] = jnp.where(first, ka, kb)
        big[slot, :NV, NV : 2 * NV] = zero
        big[slot, :NV, 2 * NV :] = r1.T
        big[slot, NV : 2 * NV, :NV] = zero
        big[slot, NV : 2 * NV, NV : 2 * NV] = jnp.where(first, kb, ka)
        big[slot, NV : 2 * NV, 2 * NV :] = r2.T
        big[slot, 2 * NV :, :NV] = r1
        big[slot, 2 * NV :, NV : 2 * NV] = r2
        big[slot, 2 * NV :, 2 * NV :] = jnp.where(eye, stiff, 0.0)

    def reduce(slots):
        ys = [dot_nn(big[i], dot_nn(big[i], start[...])) for i in slots]
        ps = chol_inv([dot_tn(y, y) for y in ys])
        images = [dot_tn(y, dot_nn(big[i], y)) for i, y in zip(slots, ys)]
        return [dot_nt(y, p) for y, p in zip(ys, ps)], [dot_nt(dot_nn(p, im), p) for p, im in zip(ps, images)]

    firsts = [ids[0] < ids[1], ids[2] < ids[3]]
    for pair in range(2):
        a, b = 2 * pair, 2 * pair + 1
        meet(pair, firsts[pair], kmat[a], rmat[0, a], kmat[b], rmat[0, b], small[a][0:1] + small[b][0:1])
    zs, ks = reduce([0, 1])
    joint = []
    for pair in range(2):
        z = zs[pair]
        lo, hi, zi = z[:NV], z[NV : 2 * NV], z[2 * NV :]
        za, zb = jnp.where(firsts[pair], lo, hi), jnp.where(firsts[pair], hi, lo)
        match = jnp.zeros((NV, NV), F32)
        for role in (2 * pair, 2 * pair + 1):
            up = jnp.sum(jnp.where(eye, small[role][3:4], 0.0), axis=1, keepdims=True)
            match = match + jnp.where(up == small[role][2:3], 1.0, 0.0)
        joint.append(
            dot_nn(rmat[1, 2 * pair], za) + dot_nn(rmat[1, 2 * pair + 1], zb) + math.sqrt(0.5) * dot_nn(match, zi)
        )
        if pair == 0:
            z_s[:NV, :] = za
            z_s[NV:, :] = zi
    first = jnp.minimum(ids[0], ids[1]) < jnp.minimum(ids[2], ids[3])
    stiff = small[0][1:2] + small[1][1:2] + small[2][1:2] + small[3][1:2]
    meet(0, first, ks[0], joint[0], ks[1], joint[1], stiff)
    (z1,), (k1,) = reduce([0])
    reduced_out[...] = k1
    top = jnp.where(first, z1[:NV], z1[NV : 2 * NV])
    at = pl.ds(pl.multiple_of(NV + h * 16, 16), 16)
    low_part = z_s[at, :]
    z_low = z_s[:NV, :]
    z_s[NV:, :] = z1[2 * NV :]
    top_part = z_s[at, :]
    final = math.sqrt(NC * 8)
    mixed = final * dot_tn(top, dot_tn(z_low, li[...]))
    spread = jnp.concatenate([math.sqrt(0.5) * final * dot_nn(low_part, top), 0.5 * final * top_part], axis=0)
    fill_hot(index, hot, F32)
    for k in range(16):
        at = slice(k * NV, (k + 1) * NV)
        part = dot_nn(mixed, w[:, at]) + dot_tn(spread, hot[:, at])
        modes_out[pl.ds(k, NV, stride=16), :] = part


def per_device(start_modes, density, planes, tree_order, iface_index, iface_stiff, reduced_start):
    row_groups = [[y * SQ + z for z in range(SQ)] for y in range(SQ)]
    col_groups = [[y * SQ + z for y in range(SQ)] for z in range(SQ)]
    chips = [[0, 2, 4, 6], [1, 3, 5, 7]]
    edge = 12 * NV + 16
    left, right = pl.pallas_call(
        prep_kernel,
        out_shape=(shape(edge, NV), shape(edge, NV)),
        in_specs=[SM, VM, VM],
        out_specs=(VM, VM),
        scratch_shapes=[pltpu.VMEM((NC, NV), F32)],
        name="prep",
        compiler_params=grant(8),
    )(planes, start_modes.reshape(NC, NV), density.reshape(16, NV))
    from_left = lax.ppermute(right, "halo", [(i, i + 1) for i in range(7)])
    from_right = lax.ppermute(left, "halo", [(i + 1, i) for i in range(7)])
    w, full, wg = pl.pallas_call(
        front_kernel,
        out_shape=(shape(NV, NC), shape(8, NV + 8, NV), shape(32, NV)),
        in_specs=[SM, SM, VM, VM, VM, VM],
        out_specs=(VM, VM, VM),
        scratch_shapes=[
            pltpu.VMEM((10, 4, 8, NV), F32),
            pltpu.VMEM((2 * NV, NC), F32),
            pltpu.VMEM((32, NC), F32),
        ],
        name="front",
        compiler_params=grant(24),
    )(planes, iface_index, left, right, from_left, from_right)
    full = lax.all_to_all(full, "halo", 0, 0, tiled=True)
    li, k_own, message = pl.pallas_call(
        own_kernel,
        out_shape=(shape(NV, NV), shape(NV, NV), shape(SQ, ROWS, NV)),
        in_specs=[VM, VM, VM, VM],
        out_specs=(VM, VM, VM),
        scratch_shapes=[pltpu.VMEM((8, NV), F32)],
        name="own",
        compiler_params=grant(8),
    )(full, wg, iface_stiff, iface_index)
    along = lax.all_to_all(message, "leaf", 0, 0, tiled=True, axis_index_groups=row_groups)
    chosen = pl.pallas_call(
        select_kernel,
        out_shape=shape(SQ, 3 * ROWS, NV),
        in_specs=[SM, VM],
        out_specs=VM,
        scratch_shapes=[pltpu.SMEM((SQ * SQ,), jnp.int32)],
        name="select",
        compiler_params=grant(4),
    )(tree_order, along)
    across = lax.all_to_all(chosen, "leaf", 0, 0, tiled=True, axis_index_groups=col_groups)
    gathered = pl.pallas_call(
        collect_kernel,
        out_shape=shape(4, AG, NV),
        in_specs=[SM, VM, VM],
        out_specs=VM,
        scratch_shapes=[pltpu.SMEM((SQ * SQ,), jnp.int32)],
        name="collect",
        compiler_params=grant(4),
    )(tree_order, across, message)
    mine = lax.all_to_all(gathered, "halo", 0, 0, tiled=True, axis_index_groups=chips)
    other = lax.ppermute(mine, "halo", [(i, i ^ 1) for i in range(8)])
    modes, reduced = pl.pallas_call(
        solve_kernel,
        out_shape=(shape(NC, NV), shape(NV, NV)),
        in_specs=[SM, SM, VM, VM, VM, VM, VM, VM],
        out_specs=(VM, VM),
        scratch_shapes=[
            pltpu.SMEM((SQ * SQ,), jnp.int32),
            pltpu.VMEM((4, NV, NV), F32),
            pltpu.VMEM((2, 4, NV, NV), F32),
            pltpu.VMEM((2, 3 * NV, 3 * NV), F32),
            pltpu.VMEM((2 * NV, NV), F32),
            pltpu.VMEM((32, NC), F32),
        ],
        name="solve",
        compiler_params=grant(20),
    )(tree_order, iface_index, mine, other, k_own, li, w, reduced_start)
    return modes.reshape(1, NV, 4, 4, NV), reduced[None]


def solution(mesh):
    return jax.shard_map(
        per_device,
        mesh=mesh,
        in_specs=(
            P("leaf", None, "halo", None, None),
            P("leaf", "halo", None, None),
            P("leaf"),
            P(),
            P("leaf", None, "halo"),
            P("leaf", None, "halo"),
            P(),
        ),
        out_specs=(P("leaf", None, "halo", None, None), P("leaf", None, None)),
        check_vma=False,
    )
```

```python
import math

import jax
import jax.numpy as jnp
from jax import lax
from jax.experimental import pallas as pl
from jax.experimental.pallas import tpu as pltpu
from jax.sharding import PartitionSpec as P

F32, BF = jnp.float32, jnp.bfloat16
HI = lax.Precision.HIGHEST
NV = 128
NC = 2048
SQ = 8
ROWS = 48
AG = 3 * ROWS + 40
VM = pl.BlockSpec(memory_space=pltpu.VMEM)
SM = pl.BlockSpec(memory_space=pltpu.SMEM)


def dot_nt(a, b):
    return lax.dot_general(a, b, (((1,), (1,)), ((), ())), precision=HI, preferred_element_type=F32)


def dot_nn(a, b):
    return lax.dot_general(a, b, (((1,), (0,)), ((), ())), precision=HI, preferred_element_type=F32)


def dot_tn(a, b):
    return lax.dot_general(a, b, (((0,), (0,)), ((), ())), precision=HI, preferred_element_type=F32)


def dot_bf(a, b):
    return lax.dot_general(a, b, (((1,), (0,)), ((), ())), preferred_element_type=F32)


def split(x):
    hi = x.astype(BF)
    return hi, (x - hi.astype(F32)).astype(BF)


def iota(shape, dim):
    return lax.broadcasted_iota(jnp.int32, shape, dim)


def grant(mib):
    return pltpu.CompilerParams(vmem_limit_bytes=mib << 20)


def shape(*dims):
    return jax.ShapeDtypeStruct(dims, F32)


def chol_inv(mats):
    count = len(mats)
    sh = (count, 8, NV)
    lane, sub = iota(sh, 2), iota(sh, 1)

    def over_lanes(x, c):
        return jnp.broadcast_to(x[:, :, c : c + 1], sh)

    def over_subs(x, r):
        return jnp.broadcast_to(x[:, r : r + 1, :], sh)

    rows = [jnp.stack([m[8 * i : 8 * i + 8, :] for m in mats]) for i in range(16)]
    for s in range(16):
        p = rows[s]
        cols = [over_lanes(p, 8 * s + j) for j in range(8)]
        scaled, scales, upper = [], [], {}
        for k in range(8):
            rs = lax.rsqrt(over_subs(cols[k], k))
            at = lane == 8 * s + k
            r = jnp.where(at, rs, over_subs(p, k) * rs)
            scaled.append(r)
            scales.append(rs)
            if k < 7:
                low = cols[k] * rs
                p = jnp.where(sub > k, jnp.where(at, 0.0, p) - low * r, p)
                for j in range(k + 1, 8):
                    upper[k, j] = over_subs(cols[j], k) * rs
                    cols[j] = cols[j] - low * upper[k, j]
        out = scaled[7]
        for k in range(7):
            out = jnp.where(sub == k, scaled[k], out)
        rows[s] = jnp.where(lane > 8 * s + sub, 0.0, out)
        inside = (lane >= 8 * s) & (lane < 8 * s + 8)
        kept = [jnp.where(inside & (lane > 8 * s + k), 0.0, scaled[k]) for k in range(8)]
        for a in range(s + 1, 16):
            q = rows[a]
            cols = [over_lanes(q, 8 * s + j) for j in range(8)]
            q = jnp.where(inside, 0.0, q)
            for k in range(8):
                low = cols[k] * scales[k]
                q = q - low * kept[k]
                for j in range(k + 1, 8):
                    cols[j] = cols[j] - low * upper[k, j]
            rows[a] = q
    return [jnp.concatenate([rows[i][b] for i in range(16)], axis=0) for b in range(count)]


def prep_kernel(planes, v, rho, left, right, wide):
    h = lax.axis_index("halo")
    wide[...] = v[...].astype(F32)
    for k in range(16):
        part = wide[pl.ds(k, NV, stride=16), :]
        part = jnp.where(h * 4 + k // 4 < planes[0], part, 0.0)
        if k < 12:
            left[k * NV : (k + 1) * NV, :] = part
        if k >= 4:
            right[(k - 4) * NV : (k - 3) * NV, :] = part
    left[12 * NV :, :] = rho[...]
    right[12 * NV : 12 * NV + 12, :] = rho[4:, :]
    right[12 * NV + 12 :, :] = rho[:4, :]


def smooth_first(cells):
    pairs = [[a + b for a, b in zip(lo, hi)] for lo, hi in zip(cells[:-1], cells[1:])]
    return [[a + b for a, b in zip(lo, hi)] for lo, hi in zip(pairs[:-1], pairs[1:])]


def smooth_second(row):
    pairs = [a + b for a, b in zip(row[:-1], row[1:])]
    return [a + b for a, b in zip([row[0]] + pairs, pairs + [row[-1]])]


def front_kernel(
    planes, index, stiff, index_v, left, right, from_left, from_right, w_out, full_out, wg_out, tile_out, rho_s, both, hot
):
    h = lax.axis_index("halo")
    tile_out[...] = jnp.zeros((8, NV), F32)
    tile_out[0:2, 0:16] = stiff[0]
    tile_out[2:4, 0:16] = (index_v[0] + h * NC).astype(F32)
    lane = iota((8, NV), 1)
    half_lo = jnp.where(lane == 0, 0.0, 0.5).astype(F32)
    half_hi = jnp.where(lane == NV - 1, 0.0, 0.5).astype(F32)
    on = [jnp.where((h * 4 + q >= 0) & (h * 4 + q < planes[0]), 1.0 / 64, 0.0) for q in range(-3, 7)]

    def place(q):
        if q < 0:
            return from_left, q + 3
        if q < 3:
            return left, q
        if q == 3:
            return right, 2
        return from_right, q - 4

    for q in range(-3, 7):
        ref, p = place(q)
        for c in range(4):
            row = 12 * NV + 4 * p + c
            rho_s[q + 3, c] = jnp.broadcast_to(ref[row : row + 1, :], (8, NV))

    def smooth_third(x):
        return x + half_lo * pltpu.roll(x, 1, 1) + half_hi * pltpu.roll(x, NV - 1, 1)

    def apply(cells, lo):
        dense = [[rho_s[lo + i, c] * x for c, x in enumerate(row)] for i, row in enumerate(cells)]
        plain, dense = smooth_first(cells), smooth_first(dense)
        out = []
        for i, (pr, dr) in enumerate(zip(plain, dense)):
            pr, dr = smooth_second(pr), smooth_second(dr)
            q = lo + 1 + i
            out.append(
                [(rho_s[q, c] * smooth_third(x) + smooth_third(y)) * on[q] for c, (x, y) in enumerate(zip(pr, dr))]
            )
        return out

    def group(g, carry):
        cells = []
        for q in range(-3, 7):
            ref, p = place(q)
            cells.append([ref[pl.ds(pl.multiple_of((4 * p + c) * NV + g * 8, 8), 8), :] for c in range(4)])
        cells = apply(apply(cells, 0), 1)
        rows = pl.ds(pl.multiple_of(g * 8, 8), 8)
        for p in range(4):
            for c in range(4):
                k = 4 * p + c
                both[rows, k * NV : (k + 1) * NV] = cells[p + 1][c]
        cells = apply(cells, 2)
        rows = pl.ds(pl.multiple_of(NV + g * 8, 8), 8)
        for p in range(4):
            for c in range(4):
                k = 4 * p + c
                both[rows, k * NV : (k + 1) * NV] = cells[p][c]
        return carry

    lax.fori_loop(0, NV // 8, group, 0)
    fill_hot(index, hot, F32)
    w = both[:NV, :]
    w_out[...] = w
    gram = dot_nt(w, both[...])
    wg_out[...] = dot_nt(hot[...], w)
    row, col = iota((NV, NV), 0), iota((NV, NV), 1)
    s, c = gram[:, :NV], gram[:, NV:]
    packed = jnp.where(row >= col, s, c)
    diag = jnp.sum(jnp.where(row == col, c, 0.0), axis=0, keepdims=True)
    for peer in range(8):
        full_out[peer, :NV, :] = packed
        full_out[peer, NV:, :] = jnp.broadcast_to(diag, (8, NV))


def fill_hot(index, hot, dtype):
    for part in range(4):
        sub = iota((8, NV), 0)
        col = jnp.zeros((8, NV), jnp.int32)
        for j in range(8):
            col = jnp.where(sub == j, index[0, part // 2, (part % 2) * 8 + j], col)
        lane = iota((8, NV), 1)
        for k in range(16):
            hot[part * 8 : part * 8 + 8, k * NV : (k + 1) * NV] = jnp.where(col == lane + k * NV, 1.0, 0.0).astype(dtype)


def own_kernel(full, wg, small, li_out, k_out, message):
    h = lax.axis_index("halo")
    total = jnp.sum(full[...], axis=0)
    packed, diag = total[:NV, :], total[NV : NV + 1, :]
    row, col = iota((NV, NV), 0), iota((NV, NV), 1)
    mirror = packed.T
    s = jnp.where(row >= col, packed, mirror)
    c = jnp.where(row < col, packed, jnp.where(row > col, mirror, diag))
    (li,) = chol_inv([s])
    k = dot_nt(dot_nn(li, c), li)
    li_out[...] = li
    k_out[...] = k
    rows = dot_nt(wg[...], li)
    lane, sub = iota((8, NV), 1), iota((8, NV), 0)
    tile = small[...]
    tile = jnp.where(sub < 4, tile, pltpu.roll(pltpu.roll(tile, NV - 8, 1), 4, 0))
    tile = pltpu.roll(tile, h * 16, 1)
    upper = k_out[pl.ds(pl.multiple_of(h * 16, 16), 8), :]
    lower = k_out[pl.ds(pl.multiple_of(h * 16 + 8, 8), 8), :]
    lower = jnp.where((lane >= h * 16) & (lane < h * 16 + 8), tile, lower)
    for peer in range(SQ):
        message[peer, :8, :] = upper
        message[peer, 8:16, :] = lower
        message[peer, 16:, :] = rows


def invert(order, inverse):
    for t in range(SQ * SQ):
        inverse[order[t]] = t


def select_kernel(order, got, out, inverse):
    odd = lax.axis_index("halo") % 2 == 1
    leaf = lax.axis_index("leaf")
    y, z = leaf // SQ, leaf % SQ
    invert(order, inverse)
    for to in range(SQ):
        position = order[jnp.where(odd, y * SQ + to, to * SQ + z)]
        for role in range(1, 4):
            source = inverse[position ^ role]
            row, col = source // SQ, source % SQ

            @pl.when(jnp.where(odd, col == z, row == y))
            def _(to=to, role=role, at=jnp.where(odd, row, col)):
                out[to, (role - 1) * ROWS : role * ROWS, :] = got[at]


def collect_kernel(order, got, message, out, inverse):
    odd = lax.axis_index("halo") % 2 == 1
    leaf = lax.axis_index("leaf")
    invert(order, inverse)
    position = order[leaf]
    parts = []
    for r in range(1, 4):
        source = inverse[position ^ r]
        parts.append(got[jnp.where(odd, source % SQ, source // SQ), (r - 1) * ROWS : r * ROWS, :])
    own = message[0, 8:, :]
    for peer in range(4):
        for r in range(3):
            out[peer, r * ROWS : (r + 1) * ROWS, :] = parts[r]
        out[peer, 3 * ROWS :, :] = own


def solve_kernel(
    order, index, mine, other, k_own, li, w, start, modes_out, reduced_out, inverse, kmat, rmat, big, z_s, hot
):
    h, leaf = lax.axis_index("halo"), lax.axis_index("leaf")
    odd = h % 2
    invert(order, inverse)
    position = order[leaf]
    ids = [leaf] + [inverse[position ^ role] for role in range(1, 4)]
    scale = 0.5 * math.sqrt(NC * 8 / NV)

    def piece(halo, lo, hi):
        a, b = mine[halo // 2, lo:hi, :], other[halo // 2, lo:hi, :]
        return jnp.where(odd == halo % 2, a, b)

    row, col = iota((NV, NV), 0), iota((NV, NV), 1)
    eye = row == col
    lane = iota((8, NV), 1)
    small = []
    kmat[0] = k_own[...]
    for role in range(4):
        base = 3 * ROWS - 8 if role == 0 else (role - 1) * ROWS
        tile = jnp.zeros((8, NV), F32)
        for halo in range(8):
            at = slice(16 * halo, 16 * halo + 16)
            lower = piece(halo, base + 8, base + 16)
            if role:
                kmat[role, 16 * halo : 16 * halo + 8, :] = piece(halo, base, base + 8)
                kmat[role, 16 * halo + 8 : 16 * halo + 16, :] = lower
            rmat[0, role, at, :] = piece(halo, base + 16, base + 32)
            rmat[1, role, at, :] = piece(halo, base + 32, base + 48)
            tile = jnp.where((lane >= 16 * halo) & (lane < 16 * halo + 8), lower, tile)
        small.append(tile + pltpu.roll(pltpu.roll(tile, 8, 1), 4, 0))
        if role:
            raw = kmat[role]
            kmat[role] = jnp.where(row <= col, raw, raw.T)

    def meet(slot, first, ka, ra, kb, rb, stiff):
        ra, rb = scale * ra, scale * rb
        r1, r2 = jnp.where(first, ra, rb), jnp.where(first, rb, ra)
        big[slot, :NV, :NV] = jnp.where(first, ka, kb)
        big[slot, :NV, NV:] = r1.T
        big[slot, NV : 2 * NV, :NV] = jnp.where(first, kb, ka)
        big[slot, NV : 2 * NV, NV:] = r2.T
        big[slot, 2 * NV :, :NV] = r1
        big[slot, 2 * NV :, NV:] = r2
        return jnp.sum(jnp.where(eye, stiff, 0.0), axis=1, keepdims=True)

    def product(slot, diag, x):
        x1, x2, x3 = x[:NV], x[NV : 2 * NV], x[2 * NV :]
        y1 = dot_nn(big[slot, :NV], jnp.concatenate([x1, x3], axis=0))
        y2 = dot_nn(big[slot, NV : 2 * NV], jnp.concatenate([x2, x3], axis=0))
        y3 = dot_nn(big[slot, 2 * NV :], x[: 2 * NV]) + diag * x3
        return jnp.concatenate([y1, y2, y3], axis=0)

    def reduce(diags):
        ys = [product(i, d, start[...]) for i, d in enumerate(diags)]
        ys = [product(i, d, y) for i, (d, y) in enumerate(zip(diags, ys))]
        ps = chol_inv([dot_tn(y, y) for y in ys])
        images = [dot_tn(y, product(i, d, y)) for i, (d, y) in enumerate(zip(diags, ys))]
        return [dot_nt(y, p) for y, p in zip(ys, ps)], [dot_nt(dot_nn(p, im), p) for p, im in zip(ps, images)]

    firsts = [ids[0] < ids[1], ids[2] < ids[3]]
    diags = []
    for pair in range(2):
        a, b = 2 * pair, 2 * pair + 1
        diag = meet(pair, firsts[pair], kmat[a], rmat[0, a], kmat[b], rmat[0, b], small[a][0:1] + small[b][0:1])
        diags.append(diag)
    zs, ks = reduce(diags)
    joint = []
    for pair in range(2):
        z = zs[pair]
        lo, hi, zi = z[:NV], z[NV : 2 * NV], z[2 * NV :]
        za, zb = jnp.where(firsts[pair], lo, hi), jnp.where(firsts[pair], hi, lo)
        match = jnp.zeros((NV, NV), F32)
        for role in (2 * pair, 2 * pair + 1):
            up = jnp.sum(jnp.where(eye, small[role][3:4], 0.0), axis=1, keepdims=True)
            match = match + jnp.where(up == small[role][2:3], 1.0, 0.0)
        joint.append(
            dot_nn(rmat[1, 2 * pair], za) + dot_nn(rmat[1, 2 * pair + 1], zb) + math.sqrt(0.5) * dot_nn(match, zi)
        )
        if pair == 0:
            z_s[:NV, :] = za
            z_s[NV:, :] = zi
    first = jnp.minimum(ids[0], ids[1]) < jnp.minimum(ids[2], ids[3])
    stiff = small[0][1:2] + small[1][1:2] + small[2][1:2] + small[3][1:2]
    diag = meet(0, first, ks[0], joint[0], ks[1], joint[1], stiff)
    (z1,), (k1,) = reduce([diag])
    reduced_out[...] = k1
    top = jnp.where(first, z1[:NV], z1[NV : 2 * NV])
    at = pl.ds(pl.multiple_of(NV + h * 16, 16), 16)
    low_part = z_s[at, :]
    z_low = z_s[:NV, :]
    z_s[NV:, :] = z1[2 * NV :]
    top_part = z_s[at, :]
    final = math.sqrt(NC * 8)
    mixed = final * dot_tn(top, dot_tn(z_low, li[...]))
    spread = jnp.concatenate([math.sqrt(0.5) * final * dot_nn(low_part, top), 0.5 * final * top_part], axis=0)
    fill_hot(index, hot, BF)
    l_hi, l_lo = split(jnp.concatenate([mixed, spread.T], axis=1))
    for k in range(0, 16, 2):
        at = slice(k * NV, (k + 2) * NV)
        r_hi, r_lo = split(w[:, at])
        tail = jnp.concatenate([r_hi, hot[:, at]], axis=0)
        part = dot_bf(l_lo, tail) + dot_bf(l_hi[:, :NV], r_lo) + dot_bf(l_hi, tail)
        modes_out[pl.ds(k, NV, stride=16), :] = part[:, :NV]
        modes_out[pl.ds(k + 1, NV, stride=16), :] = part[:, NV:]


def per_device(start_modes, density, planes, tree_order, iface_index, iface_stiff, reduced_start):
    rows = [[h * 64 + y * SQ + z for z in range(SQ)] for h in range(8) for y in range(SQ)]
    cols = [[h * 64 + y * SQ + z for y in range(SQ)] for h in range(8) for z in range(SQ)]
    even = [h % 2 == 0 for h in range(8) for _ in range(SQ)]
    first_groups = [r if e else c for e, r, c in zip(even, rows, cols)]
    second_groups = [c if e else r for e, r, c in zip(even, rows, cols)]
    everyone = ("halo", "leaf")
    chips = [[0, 2, 4, 6], [1, 3, 5, 7]]
    edge = 12 * NV + 16
    left, right = pl.pallas_call(
        prep_kernel,
        out_shape=(shape(edge, NV), shape(edge, NV)),
        in_specs=[SM, VM, VM],
        out_specs=(VM, VM),
        scratch_shapes=[pltpu.VMEM((NC, NV), F32)],
        name="prep",
        compiler_params=grant(8),
    )(planes, start_modes.reshape(NC, NV), density.reshape(16, NV))
    from_left = lax.ppermute(right, "halo", [(i, i + 1) for i in range(7)])
    from_right = lax.ppermute(left, "halo", [(i + 1, i) for i in range(7)])
    w, full, wg, small = pl.pallas_call(
        front_kernel,
        out_shape=(shape(NV, NC), shape(8, NV + 8, NV), shape(32, NV), shape(8, NV)),
        in_specs=[SM, SM, VM, VM, VM, VM, VM, VM],
        out_specs=(VM, VM, VM, VM),
        scratch_shapes=[
            pltpu.VMEM((10, 4, 8, NV), F32),
            pltpu.VMEM((2 * NV, NC), F32),
            pltpu.VMEM((32, NC), F32),
        ],
        name="front",
        compiler_params=grant(24),
    )(planes, iface_index, iface_stiff, iface_index, left, right, from_left, from_right)
    full = lax.all_to_all(full, "halo", 0, 0, tiled=True)
    li, k_own, message = pl.pallas_call(
        own_kernel,
        out_shape=(shape(NV, NV), shape(NV, NV), shape(SQ, ROWS, NV)),
        in_specs=[VM, VM, VM],
        out_specs=(VM, VM, VM),
        name="own",
        compiler_params=grant(8),
    )(full, wg, small)
    along = lax.all_to_all(message, everyone, 0, 0, tiled=True, axis_index_groups=first_groups)
    chosen = pl.pallas_call(
        select_kernel,
        out_shape=shape(SQ, 3 * ROWS, NV),
        in_specs=[SM, VM],
        out_specs=VM,
        scratch_shapes=[pltpu.SMEM((SQ * SQ,), jnp.int32)],
        name="select",
        compiler_params=grant(4),
    )(tree_order, along)
    across = lax.all_to_all(chosen, everyone, 0, 0, tiled=True, axis_index_groups=second_groups)
    gathered = pl.pallas_call(
        collect_kernel,
        out_shape=shape(4, AG, NV),
        in_specs=[SM, VM, VM],
        out_specs=VM,
        scratch_shapes=[pltpu.SMEM((SQ * SQ,), jnp.int32)],
        name="collect",
        compiler_params=grant(4),
    )(tree_order, across, message)
    mine = lax.all_to_all(gathered, "halo", 0, 0, tiled=True, axis_index_groups=chips)
    other = lax.ppermute(mine, "halo", [(i, i ^ 1) for i in range(8)])
    modes, reduced = pl.pallas_call(
        solve_kernel,
        out_shape=(shape(NC, NV), shape(NV, NV)),
        in_specs=[SM, SM, VM, VM, VM, VM, VM, VM],
        out_specs=(VM, VM),
        scratch_shapes=[
            pltpu.SMEM((SQ * SQ,), jnp.int32),
            pltpu.VMEM((4, NV, NV), F32),
            pltpu.VMEM((2, 4, NV, NV), F32),
            pltpu.VMEM((2, 3 * NV, 2 * NV), F32),
            pltpu.VMEM((2 * NV, NV), F32),
            pltpu.VMEM((32, NC), BF),
        ],
        name="solve",
        compiler_params=grant(20),
    )(tree_order, iface_index, mine, other, k_own, li, w, reduced_start)
    return modes.reshape(1, NV, 4, 4, NV), reduced[None]


def solution(mesh):
    return jax.shard_map(
        per_device,
        mesh=mesh,
        in_specs=(
            P("leaf", None, "halo", None, None),
            P("leaf", "halo", None, None),
            P("leaf"),
            P(),
            P("leaf", None, "halo"),
            P("leaf", None, "halo"),
            P(),
        ),
        out_specs=(P("leaf", None, "halo", None, None), P("leaf", None, None)),
        check_vma=False,
    )
```

```python
import math

import jax
import jax.numpy as jnp
from jax import lax
from jax.experimental import pallas as pl
from jax.experimental.pallas import tpu as pltpu
from jax.sharding import PartitionSpec as P

F32, BF = jnp.float32, jnp.bfloat16
HI = lax.Precision.HIGHEST
NV = 128
NC = 2048
SQ = 8
ROWS = 48
AG = 3 * ROWS + 40
VM = pl.BlockSpec(memory_space=pltpu.VMEM)
SM = pl.BlockSpec(memory_space=pltpu.SMEM)
FAR = pl.BlockSpec(memory_space=pltpu.HBM)


def dot_nt(a, b):
    return lax.dot_general(a, b, (((1,), (1,)), ((), ())), precision=HI, preferred_element_type=F32)


def dot_nn(a, b):
    return lax.dot_general(a, b, (((1,), (0,)), ((), ())), precision=HI, preferred_element_type=F32)


def dot_tn(a, b):
    return lax.dot_general(a, b, (((0,), (0,)), ((), ())), precision=HI, preferred_element_type=F32)


def dot_bf(a, b):
    return lax.dot_general(a, b, (((1,), (0,)), ((), ())), preferred_element_type=F32)


def split(x):
    hi = x.astype(BF)
    return hi, (x - hi.astype(F32)).astype(BF)


def iota(shape, dim):
    return lax.broadcasted_iota(jnp.int32, shape, dim)


def far(x):
    return pltpu.with_memory_space_constraint(x, pltpu.HBM)


def grant(mib):
    return pltpu.CompilerParams(vmem_limit_bytes=mib << 20)


def shape(*dims):
    return jax.ShapeDtypeStruct(dims, F32)


def eliminate(mats):
    count, width = len(mats), mats[0].shape[1]
    n = width // 8
    sh = (count, 8, width)
    lane, sub = iota(sh, 2), iota(sh, 1)

    def over_lanes(x, c):
        return jnp.broadcast_to(x[:, :, c : c + 1], sh)

    def over_subs(x, r):
        return jnp.broadcast_to(x[:, r : r + 1, :], sh)

    rows = [jnp.stack([m[8 * i : 8 * i + 8, :] for m in mats]) for i in range(n)]
    ready = [over_lanes(rows[0], j) for j in range(8)]
    for s in range(n):
        p, cols = rows[s], ready
        inside = (lane >= 8 * s) & (lane < 8 * s + 8)
        after = s + 1 < n
        if after:
            q = rows[s + 1]
            mine = [over_lanes(q, 8 * s + j) for j in range(8)]
            ready = [over_lanes(q, 8 * s + 8 + j) for j in range(8)]
            q = jnp.where(inside, 0.0, q)
        scaled, kept, scales, upper = [], [], [], {}
        for k in range(8):
            rs = lax.rsqrt(over_subs(cols[k], k))
            at = lane == 8 * s + k
            r = jnp.where(at, rs, over_subs(p, k) * rs)
            scaled.append(r)
            scales.append(rs)
            kept.append(jnp.where(inside & (lane > 8 * s + k), 0.0, r))
            if k < 7:
                low = cols[k] * rs
                for j in range(k + 1, 8):
                    upper[k, j] = over_subs(cols[j], k) * rs
                    cols[j] = cols[j] - low * upper[k, j]
                p = jnp.where(sub > k, jnp.where(at, 0.0, p) - low * r, p)
            if after:
                low = mine[k] * rs
                for j in range(k + 1, 8):
                    mine[j] = mine[j] - low * upper[k, j]
                for j in range(8):
                    ready[j] = ready[j] - low * over_subs(low, j)
                q = q - low * kept[k]
        out = scaled[7]
        for k in range(7):
            out = jnp.where(sub == k, scaled[k], out)
        rows[s] = jnp.where(lane > 8 * s + sub, 0.0, out)
        if after:
            rows[s + 1] = q
        for a in range(s + 2, n):
            q = rows[a]
            cols = [over_lanes(q, 8 * s + j) for j in range(8)]
            q = jnp.where(inside, 0.0, q)
            for k in range(8):
                low = cols[k] * scales[k]
                q = q - low * kept[k]
                for j in range(k + 1, 8):
                    cols[j] = cols[j] - low * upper[k, j]
            rows[a] = q
    return [jnp.concatenate([rows[i][b] for i in range(n)], axis=0) for b in range(count)]


def chol_inv(mats):
    if len(mats) == 1:
        return eliminate(mats)
    half = NV // 2
    tops = eliminate([m[:half, :half] for m in mats])
    sides = [dot_nt(m[half:, :half], t) for m, t in zip(mats, tops)]
    ends = eliminate([m[half:, half:] - dot_nt(x, x) for m, x in zip(mats, sides)])
    lows = [dot_nn(e, dot_nn(x, t)) for x, t, e in zip(sides, tops, ends)]
    zero = jnp.zeros((half, half), F32)
    return [
        jnp.concatenate([jnp.concatenate([t, zero], axis=1), jnp.concatenate([-x, e], axis=1)], axis=0)
        for t, x, e in zip(tops, lows, ends)
    ]


def prep_kernel(planes, v_far, rho_far, left, right, v, wide, rho, sems):
    h = lax.axis_index("halo")
    step = NC // 4
    copies = [
        pltpu.make_async_copy(v_far.at[i * step : (i + 1) * step], v.at[i * step : (i + 1) * step], sems.at[i])
        for i in range(4)
    ]
    copies.append(pltpu.make_async_copy(rho_far, rho, sems.at[4]))
    for copy in copies:
        copy.start()
    for i in range(4):
        copies[i].wait()
        wide[i * step : (i + 1) * step, :] = v[i * step : (i + 1) * step, :].astype(F32)
        for k in range(16):
            part = wide[pl.ds(i * step + k, NV // 4, stride=16), :]
            part = jnp.where(h * 4 + k // 4 < planes[0], part, 0.0)
            at = k * NV + i * (NV // 4)
            if k < 12:
                left[at : at + NV // 4, :] = part
            if k >= 4:
                right[at - 4 * NV : at - 4 * NV + NV // 4, :] = part
    copies[4].wait()
    left[12 * NV :, :] = rho[...]
    right[12 * NV : 12 * NV + 12, :] = rho[4:, :]
    right[12 * NV + 12 :, :] = rho[:4, :]


def smooth_first(cells):
    pairs = [[a + b for a, b in zip(lo, hi)] for lo, hi in zip(cells[:-1], cells[1:])]
    return [[a + b for a, b in zip(lo, hi)] for lo, hi in zip(pairs[:-1], pairs[1:])]


def smooth_second(row):
    pairs = [a + b for a, b in zip(row[:-1], row[1:])]
    return [a + b for a, b in zip([row[0]] + pairs, pairs + [row[-1]])]


def front_kernel(
    planes, index, stiff, index_v, left, right, from_left, from_right, w_out, full_out, wg_out, tile_out, rho_s, both, acc
):
    h = lax.axis_index("halo")
    tile_out[...] = jnp.zeros((8, NV), F32)
    tile_out[0:2, 0:16] = stiff[0]
    tile_out[2:4, 0:16] = (index_v[0] + h * NC).astype(F32)
    lane = iota((8, NV), 1)
    half_lo = jnp.where(lane == 0, 0.0, 0.5).astype(F32)
    half_hi = jnp.where(lane == NV - 1, 0.0, 0.5).astype(F32)
    on = [jnp.where((h * 4 + q >= 0) & (h * 4 + q < planes[0]), 1.0 / 64, 0.0) for q in range(-3, 7)]

    def place(q):
        if q < 0:
            return from_left, q + 3
        if q < 3:
            return left, q
        if q == 3:
            return right, 2
        return from_right, q - 4

    for q in range(-3, 7):
        ref, p = place(q)
        for c in range(4):
            row = 12 * NV + 4 * p + c
            rho_s[q + 3, c] = jnp.broadcast_to(ref[row : row + 1, :], (8, NV))

    def smooth_third(x):
        return x + half_lo * pltpu.roll(x, 1, 1) + half_hi * pltpu.roll(x, NV - 1, 1)

    def apply(cells, lo):
        dense = [[rho_s[lo + i, c] * x for c, x in enumerate(row)] for i, row in enumerate(cells)]
        plain, dense = smooth_first(cells), smooth_first(dense)
        out = []
        for i, (pr, dr) in enumerate(zip(plain, dense)):
            pr, dr = smooth_second(pr), smooth_second(dr)
            q = lo + 1 + i
            out.append(
                [(rho_s[q, c] * smooth_third(x) + smooth_third(y)) * on[q] for c, (x, y) in enumerate(zip(pr, dr))]
            )
        return out

    def group(g, carry):
        cells = []
        for q in range(-3, 7):
            ref, p = place(q)
            cells.append([ref[pl.ds(pl.multiple_of((4 * p + c) * NV + g * 8, 8), 8), :] for c in range(4)])
        cells = apply(apply(cells, 0), 1)
        rows = pl.ds(pl.multiple_of(32 + g * 8, 8), 8)
        for p in range(4):
            for c in range(4):
                k = 4 * p + c
                both[rows, k * NV : (k + 1) * NV] = cells[p + 1][c]
        cells = apply(cells, 2)
        rows = pl.ds(pl.multiple_of(32 + NV + g * 8, 8), 8)
        for p in range(4):
            for c in range(4):
                k = 4 * p + c
                both[rows, k * NV : (k + 1) * NV] = cells[p][c]
        return carry

    lax.fori_loop(0, NV // 8, group, 0)
    fill_hot(index, both, F32)
    w_out[...] = both[32 : 32 + NV, :]
    acc[...] = jnp.zeros((32 + NV, 2 * NV), F32)

    def chunk(i, carry):
        at = pl.ds(pl.multiple_of(i * 256, 256), 256)
        acc[...] += dot_nt(both[: 32 + NV, at], both[32:, at])
        return carry

    lax.fori_loop(0, NC // 256, chunk, 0)
    wg_out[...] = acc[:32, :NV]
    row, col = iota((NV, NV), 0), iota((NV, NV), 1)
    s, c = acc[32:, :NV], acc[32:, NV:]
    packed = jnp.where(row >= col, s, c)
    diag = jnp.sum(jnp.where(row == col, c, 0.0), axis=0, keepdims=True)
    for peer in range(8):
        full_out[peer, :NV, :] = packed
        full_out[peer, NV:, :] = jnp.broadcast_to(diag, (8, NV))


def fill_hot(index, hot, dtype):
    for part in range(4):
        sub = iota((8, NV), 0)
        col = jnp.zeros((8, NV), jnp.int32)
        for j in range(8):
            col = jnp.where(sub == j, index[0, part // 2, (part % 2) * 8 + j], col)
        lane = iota((8, NV), 1)
        for k in range(16):
            hot[part * 8 : part * 8 + 8, k * NV : (k + 1) * NV] = jnp.where(col == lane + k * NV, 1.0, 0.0).astype(dtype)


def own_kernel(full, wg, small, li_out, k_out, message):
    h = lax.axis_index("halo")
    total = jnp.sum(full[...], axis=0)
    packed, diag = total[:NV, :], total[NV : NV + 1, :]
    row, col = iota((NV, NV), 0), iota((NV, NV), 1)
    mirror = packed.T
    s = jnp.where(row >= col, packed, mirror)
    c = jnp.where(row < col, packed, jnp.where(row > col, mirror, diag))
    (li,) = chol_inv([s])
    k = dot_nt(dot_nn(li, c), li)
    li_out[...] = li
    k_out[...] = k
    rows = dot_nt(wg[...], li)
    lane, sub = iota((8, NV), 1), iota((8, NV), 0)
    tile = small[...]
    tile = jnp.where(sub < 4, tile, pltpu.roll(pltpu.roll(tile, NV - 8, 1), 4, 0))
    tile = pltpu.roll(tile, h * 16, 1)
    upper = k_out[pl.ds(pl.multiple_of(h * 16, 16), 8), :]
    lower = k_out[pl.ds(pl.multiple_of(h * 16 + 8, 8), 8), :]
    lower = jnp.where((lane >= h * 16) & (lane < h * 16 + 8), tile, lower)
    for peer in range(SQ):
        message[peer, :8, :] = upper
        message[peer, 8:16, :] = lower
        message[peer, 16:, :] = rows


def invert(order, inverse):
    for t in range(SQ * SQ):
        inverse[order[t]] = t


def select_kernel(order, got, out, inverse):
    odd = lax.axis_index("halo") % 2 == 1
    leaf = lax.axis_index("leaf")
    y, z = leaf // SQ, leaf % SQ
    invert(order, inverse)
    for to in range(SQ):
        position = order[jnp.where(odd, y * SQ + to, to * SQ + z)]
        for role in range(1, 4):
            source = inverse[position ^ role]
            row, col = source // SQ, source % SQ

            @pl.when(jnp.where(odd, col == z, row == y))
            def _(to=to, role=role, at=jnp.where(odd, row, col)):
                out[to, (role - 1) * ROWS : role * ROWS, :] = got[at]


def collect_kernel(order, got, message, out, inverse):
    odd = lax.axis_index("halo") % 2 == 1
    leaf = lax.axis_index("leaf")
    invert(order, inverse)
    position = order[leaf]
    parts = []
    for r in range(1, 4):
        source = inverse[position ^ r]
        parts.append(got[jnp.where(odd, source % SQ, source // SQ), (r - 1) * ROWS : r * ROWS, :])
    own = message[0, 8:, :]
    for peer in range(4):
        for r in range(3):
            out[peer, r * ROWS : (r + 1) * ROWS, :] = parts[r]
        out[peer, 3 * ROWS :, :] = own


def solve_kernel(
    order, index, mine, other, k_own, li, w, start, modes_out, reduced_out, inverse, kmat, rmat, big, z_s, hot
):
    h, leaf = lax.axis_index("halo"), lax.axis_index("leaf")
    odd = h % 2
    invert(order, inverse)
    position = order[leaf]
    ids = [leaf] + [inverse[position ^ role] for role in range(1, 4)]
    scale = 0.5 * math.sqrt(NC * 8 / NV)

    def piece(halo, lo, hi):
        a, b = mine[halo // 2, lo:hi, :], other[halo // 2, lo:hi, :]
        return jnp.where(odd == halo % 2, a, b)

    row, col = iota((NV, NV), 0), iota((NV, NV), 1)
    eye = row == col
    lane = iota((8, NV), 1)
    small = []
    kmat[0] = k_own[...]
    for role in range(4):
        base = 3 * ROWS - 8 if role == 0 else (role - 1) * ROWS
        tile = jnp.zeros((8, NV), F32)
        for halo in range(8):
            at = slice(16 * halo, 16 * halo + 16)
            lower = piece(halo, base + 8, base + 16)
            if role:
                kmat[role, 16 * halo : 16 * halo + 8, :] = piece(halo, base, base + 8)
                kmat[role, 16 * halo + 8 : 16 * halo + 16, :] = lower
            rmat[0, role, at, :] = piece(halo, base + 16, base + 32)
            rmat[1, role, at, :] = piece(halo, base + 32, base + 48)
            tile = jnp.where((lane >= 16 * halo) & (lane < 16 * halo + 8), lower, tile)
        small.append(tile + pltpu.roll(pltpu.roll(tile, 8, 1), 4, 0))
        if role:
            raw = kmat[role]
            kmat[role] = jnp.where(row <= col, raw, raw.T)

    def meet(slot, first, ka, ra, kb, rb, stiff):
        ra, rb = scale * ra, scale * rb
        r1, r2 = jnp.where(first, ra, rb), jnp.where(first, rb, ra)
        big[slot, :NV, :NV] = jnp.where(first, ka, kb)
        big[slot, :NV, NV:] = r1.T
        big[slot, NV : 2 * NV, :NV] = jnp.where(first, kb, ka)
        big[slot, NV : 2 * NV, NV:] = r2.T
        big[slot, 2 * NV :, :NV] = r1
        big[slot, 2 * NV :, NV:] = r2
        return jnp.sum(jnp.where(eye, stiff, 0.0), axis=1, keepdims=True)

    def product(slot, diag, x):
        x1, x2, x3 = x[:NV], x[NV : 2 * NV], x[2 * NV :]
        y1 = dot_nn(big[slot, :NV], jnp.concatenate([x1, x3], axis=0))
        y2 = dot_nn(big[slot, NV : 2 * NV], jnp.concatenate([x2, x3], axis=0))
        y3 = dot_nn(big[slot, 2 * NV :], x[: 2 * NV]) + diag * x3
        return jnp.concatenate([y1, y2, y3], axis=0)

    def reduce(diags):
        ys = [product(i, d, start[...]) for i, d in enumerate(diags)]
        ys = [product(i, d, y) for i, (d, y) in enumerate(zip(diags, ys))]
        ps = chol_inv([dot_tn(y, y) for y in ys])
        images = [dot_tn(y, product(i, d, y)) for i, (d, y) in enumerate(zip(diags, ys))]
        return [dot_nt(y, p) for y, p in zip(ys, ps)], [dot_nt(dot_nn(p, im), p) for p, im in zip(ps, images)]

    firsts = [ids[0] < ids[1], ids[2] < ids[3]]
    diags = []
    for pair in range(2):
        a, b = 2 * pair, 2 * pair + 1
        diag = meet(pair, firsts[pair], kmat[a], rmat[0, a], kmat[b], rmat[0, b], small[a][0:1] + small[b][0:1])
        diags.append(diag)
    zs, ks = reduce(diags)
    joint = []
    for pair in range(2):
        z = zs[pair]
        lo, hi, zi = z[:NV], z[NV : 2 * NV], z[2 * NV :]
        za, zb = jnp.where(firsts[pair], lo, hi), jnp.where(firsts[pair], hi, lo)
        match = jnp.zeros((NV, NV), F32)
        for role in (2 * pair, 2 * pair + 1):
            up = jnp.sum(jnp.where(eye, small[role][3:4], 0.0), axis=1, keepdims=True)
            match = match + jnp.where(up == small[role][2:3], 1.0, 0.0)
        joint.append(
            dot_nn(rmat[1, 2 * pair], za) + dot_nn(rmat[1, 2 * pair + 1], zb) + math.sqrt(0.5) * dot_nn(match, zi)
        )
        if pair == 0:
            z_s[:NV, :] = za
            z_s[NV:, :] = zi
    first = jnp.minimum(ids[0], ids[1]) < jnp.minimum(ids[2], ids[3])
    stiff = small[0][1:2] + small[1][1:2] + small[2][1:2] + small[3][1:2]
    diag = meet(0, first, ks[0], joint[0], ks[1], joint[1], stiff)
    (z1,), (k1,) = reduce([diag])
    reduced_out[...] = k1
    top = jnp.where(first, z1[:NV], z1[NV : 2 * NV])
    at = pl.ds(pl.multiple_of(NV + h * 16, 16), 16)
    low_part = z_s[at, :]
    z_low = z_s[:NV, :]
    z_s[NV:, :] = z1[2 * NV :]
    top_part = z_s[at, :]
    final = math.sqrt(NC * 8)
    mixed = final * dot_tn(top, dot_tn(z_low, li[...]))
    spread = jnp.concatenate([math.sqrt(0.5) * final * dot_nn(low_part, top), 0.5 * final * top_part], axis=0)
    fill_hot(index, hot, BF)
    l_hi, l_lo = split(jnp.concatenate([mixed, spread.T], axis=1))
    for k in range(0, 16, 2):
        at = slice(k * NV, (k + 2) * NV)
        r_hi, r_lo = split(w[:, at])
        tail = jnp.concatenate([r_hi, hot[:, at]], axis=0)
        part = dot_bf(l_lo, tail) + dot_bf(l_hi[:, :NV], r_lo) + dot_bf(l_hi, tail)
        modes_out[pl.ds(k, NV, stride=16), :] = part[:, :NV]
        modes_out[pl.ds(k + 1, NV, stride=16), :] = part[:, NV:]


def per_device(start_modes, density, planes, tree_order, iface_index, iface_stiff, reduced_start):
    rows = [[h * 64 + y * SQ + z for z in range(SQ)] for h in range(8) for y in range(SQ)]
    cols = [[h * 64 + y * SQ + z for y in range(SQ)] for h in range(8) for z in range(SQ)]
    even = [h % 2 == 0 for h in range(8) for _ in range(SQ)]
    first_groups = [r if e else c for e, r, c in zip(even, rows, cols)]
    second_groups = [c if e else r for e, r, c in zip(even, rows, cols)]
    everyone = ("halo", "leaf")
    chips = [[0, 2, 4, 6], [1, 3, 5, 7]]
    edge = 12 * NV + 16
    left, right = pl.pallas_call(
        prep_kernel,
        out_shape=(shape(edge, NV), shape(edge, NV)),
        in_specs=[SM, FAR, FAR],
        out_specs=(VM, VM),
        scratch_shapes=[
            pltpu.VMEM((NC, NV), BF),
            pltpu.VMEM((NC, NV), F32),
            pltpu.VMEM((16, NV), F32),
            pltpu.SemaphoreType.DMA((5,)),
        ],
        name="prep",
        compiler_params=grant(8),
    )(planes, far(start_modes.reshape(NC, NV)), far(density.reshape(16, NV)))
    from_left = lax.ppermute(right, "halo", [(i, i + 1) for i in range(7)])
    from_right = lax.ppermute(left, "halo", [(i + 1, i) for i in range(7)])
    w, full, wg, small = pl.pallas_call(
        front_kernel,
        out_shape=(shape(NV, NC), shape(8, NV + 8, NV), shape(32, NV), shape(8, NV)),
        in_specs=[SM, SM, VM, VM, VM, VM, VM, VM],
        out_specs=(VM, VM, VM, VM),
        scratch_shapes=[
            pltpu.VMEM((10, 4, 8, NV), F32),
            pltpu.VMEM((32 + 2 * NV, NC), F32),
            pltpu.VMEM((32 + NV, 2 * NV), F32),
        ],
        name="front",
        compiler_params=grant(24),
    )(planes, iface_index, iface_stiff, iface_index, left, right, from_left, from_right)
    full = lax.all_to_all(full, "halo", 0, 0, tiled=True)
    li, k_own, message = pl.pallas_call(
        own_kernel,
        out_shape=(shape(NV, NV), shape(NV, NV), shape(SQ, ROWS, NV)),
        in_specs=[VM, VM, VM],
        out_specs=(VM, VM, VM),
        name="own",
        compiler_params=grant(8),
    )(full, wg, small)
    along = lax.all_to_all(message, everyone, 0, 0, tiled=True, axis_index_groups=first_groups)
    chosen = pl.pallas_call(
        select_kernel,
        out_shape=shape(SQ, 3 * ROWS, NV),
        in_specs=[SM, VM],
        out_specs=VM,
        scratch_shapes=[pltpu.SMEM((SQ * SQ,), jnp.int32)],
        name="select",
        compiler_params=grant(4),
    )(tree_order, along)
    across = lax.all_to_all(chosen, everyone, 0, 0, tiled=True, axis_index_groups=second_groups)
    gathered = pl.pallas_call(
        collect_kernel,
        out_shape=shape(4, AG, NV),
        in_specs=[SM, VM, VM],
        out_specs=VM,
        scratch_shapes=[pltpu.SMEM((SQ * SQ,), jnp.int32)],
        name="collect",
        compiler_params=grant(4),
    )(tree_order, across, message)
    mine = lax.all_to_all(gathered, "halo", 0, 0, tiled=True, axis_index_groups=chips)
    other = lax.ppermute(mine, "halo", [(i, i ^ 1) for i in range(8)])
    modes, reduced = pl.pallas_call(
        solve_kernel,
        out_shape=(shape(NC, NV), shape(NV, NV)),
        in_specs=[SM, SM, VM, VM, VM, VM, VM, VM],
        out_specs=(VM, VM),
        scratch_shapes=[
            pltpu.SMEM((SQ * SQ,), jnp.int32),
            pltpu.VMEM((4, NV, NV), F32),
            pltpu.VMEM((2, 4, NV, NV), F32),
            pltpu.VMEM((2, 3 * NV, 2 * NV), F32),
            pltpu.VMEM((2 * NV, NV), F32),
            pltpu.VMEM((32, NC), BF),
        ],
        name="solve",
        compiler_params=grant(20),
    )(tree_order, iface_index, mine, other, k_own, li, w, reduced_start)
    return modes.reshape(1, NV, 4, 4, NV), reduced[None]


def solution(mesh):
    return jax.shard_map(
        per_device,
        mesh=mesh,
        in_specs=(
            P("leaf", None, "halo", None, None),
            P("leaf", "halo", None, None),
            P("leaf"),
            P(),
            P("leaf", None, "halo"),
            P("leaf", None, "halo"),
            P(),
        ),
        out_specs=(P("leaf", None, "halo", None, None), P("leaf", None, None)),
        check_vma=False,
    )
```

```python
import math

import jax
import jax.numpy as jnp
from jax import lax
from jax.experimental import pallas as pl
from jax.experimental.pallas import tpu as pltpu
from jax.sharding import PartitionSpec as P

F32, BF = jnp.float32, jnp.bfloat16
HI = lax.Precision.HIGHEST
NV = 128
NC = 2048
SQ = 8
ROWS = 48
AG = 3 * ROWS + 40
VM = pl.BlockSpec(memory_space=pltpu.VMEM)
SM = pl.BlockSpec(memory_space=pltpu.SMEM)
FAR = pl.BlockSpec(memory_space=pltpu.HBM)


def dot_nt(a, b):
    return lax.dot_general(a, b, (((1,), (1,)), ((), ())), precision=HI, preferred_element_type=F32)


def dot_nn(a, b):
    return lax.dot_general(a, b, (((1,), (0,)), ((), ())), precision=HI, preferred_element_type=F32)


def dot_tn(a, b):
    return lax.dot_general(a, b, (((0,), (0,)), ((), ())), precision=HI, preferred_element_type=F32)


def dot_bf(a, b):
    return lax.dot_general(a, b, (((1,), (0,)), ((), ())), preferred_element_type=F32)


def split(x):
    hi = x.astype(BF)
    return hi, (x - hi.astype(F32)).astype(BF)


def iota(shape, dim):
    return lax.broadcasted_iota(jnp.int32, shape, dim)


def far(x):
    return pltpu.with_memory_space_constraint(x, pltpu.HBM)


def grant(mib):
    return pltpu.CompilerParams(vmem_limit_bytes=mib << 20)


def shape(*dims):
    return jax.ShapeDtypeStruct(dims, F32)


def eliminate(mats):
    side = len(mats)
    width = NV // side
    n = width // 8
    sh = (8, NV)
    lane, sub = iota(sh, 1), iota(sh, 0)
    base = lane - lane % width
    lane = lane - base

    def over_lanes(x, c):
        if side == 1:
            return jnp.broadcast_to(x[:, c : c + 1], sh)
        return jnp.take_along_axis(x, base + c, axis=1)

    def over_subs(x, r):
        return jnp.broadcast_to(x[r : r + 1, :], sh)

    whole = jnp.concatenate(mats, axis=1) if side > 1 else mats[0]
    rows = [whole[8 * i : 8 * i + 8, :] for i in range(n)]
    ready = [over_lanes(rows[0], j) for j in range(8)]
    for s in range(n):
        p, cols = rows[s], ready
        inside = (lane >= 8 * s) & (lane < 8 * s + 8)
        after = s + 1 < n
        if after:
            q = rows[s + 1]
            mine = [over_lanes(q, 8 * s + j) for j in range(8)]
            ready = [over_lanes(q, 8 * s + 8 + j) for j in range(8)]
            q = jnp.where(inside, 0.0, q)
        scaled, kept, scales, upper = [], [], [], {}
        for k in range(8):
            rs = lax.rsqrt(over_subs(cols[k], k))
            at = lane == 8 * s + k
            r = jnp.where(at, rs, over_subs(p, k) * rs)
            scaled.append(r)
            scales.append(rs)
            kept.append(jnp.where(inside & (lane > 8 * s + k), 0.0, r))
            if k < 7:
                low = cols[k] * rs
                for j in range(k + 1, 8):
                    upper[k, j] = over_subs(cols[j], k) * rs
                    cols[j] = cols[j] - low * upper[k, j]
                p = jnp.where(sub > k, jnp.where(at, 0.0, p) - low * r, p)
            if after:
                low = mine[k] * rs
                for j in range(k + 1, 8):
                    mine[j] = mine[j] - low * upper[k, j]
                for j in range(8):
                    ready[j] = ready[j] - low * over_subs(low, j)
                q = q - low * kept[k]
        out = scaled[7]
        for k in range(7):
            out = jnp.where(sub == k, scaled[k], out)
        rows[s] = jnp.where(lane > 8 * s + sub, 0.0, out)
        if after:
            rows[s + 1] = q
        for a in range(s + 2, n):
            q = rows[a]
            cols = [over_lanes(q, 8 * s + j) for j in range(8)]
            q = jnp.where(inside, 0.0, q)
            for k in range(8):
                low = cols[k] * scales[k]
                q = q - low * kept[k]
                for j in range(k + 1, 8):
                    cols[j] = cols[j] - low * upper[k, j]
            rows[a] = q
    whole = jnp.concatenate(rows, axis=0)
    return [whole[:, width * b : width * (b + 1)] for b in range(side)]


def chol_inv(mats):
    if len(mats) == 1:
        return eliminate(mats)
    half = NV // 2
    tops = eliminate([m[:half, :half] for m in mats])
    sides = [dot_nt(m[half:, :half], t) for m, t in zip(mats, tops)]
    ends = eliminate([m[half:, half:] - dot_nt(x, x) for m, x in zip(mats, sides)])
    lows = [dot_nn(e, dot_nn(x, t)) for x, t, e in zip(sides, tops, ends)]
    zero = jnp.zeros((half, half), F32)
    return [
        jnp.concatenate([jnp.concatenate([t, zero], axis=1), jnp.concatenate([-x, e], axis=1)], axis=0)
        for t, x, e in zip(tops, lows, ends)
    ]


def prep_kernel(planes, v_far, rho_far, left, right, v, wide, rho, sems):
    h = lax.axis_index("halo")
    step = NC // 4
    copies = [
        pltpu.make_async_copy(v_far.at[i * step : (i + 1) * step], v.at[i * step : (i + 1) * step], sems.at[i])
        for i in range(4)
    ]
    copies.append(pltpu.make_async_copy(rho_far, rho, sems.at[4]))
    for copy in copies:
        copy.start()
    for i in range(4):
        copies[i].wait()
        wide[i * step : (i + 1) * step, :] = v[i * step : (i + 1) * step, :].astype(F32)
        for k in range(16):
            part = wide[pl.ds(i * step + k, NV // 4, stride=16), :]
            part = jnp.where(h * 4 + k // 4 < planes[0], part, 0.0)
            at = k * NV + i * (NV // 4)
            if k < 12:
                left[at : at + NV // 4, :] = part
            if k >= 4:
                right[at - 4 * NV : at - 4 * NV + NV // 4, :] = part
    copies[4].wait()
    left[12 * NV :, :] = rho[...]
    right[12 * NV : 12 * NV + 12, :] = rho[4:, :]
    right[12 * NV + 12 :, :] = rho[:4, :]


def smooth_first(cells):
    pairs = [[a + b for a, b in zip(lo, hi)] for lo, hi in zip(cells[:-1], cells[1:])]
    return [[a + b for a, b in zip(lo, hi)] for lo, hi in zip(pairs[:-1], pairs[1:])]


def smooth_second(row):
    pairs = [a + b for a, b in zip(row[:-1], row[1:])]
    return [a + b for a, b in zip([row[0]] + pairs, pairs + [row[-1]])]


def front_kernel(
    planes, index, stiff, index_v, left, right, from_left, from_right, w_out, full_out, wg_out, tile_out, rho_s, both
):
    h = lax.axis_index("halo")
    tile_out[...] = jnp.zeros((8, NV), F32)
    tile_out[0:2, 0:16] = stiff[0]
    tile_out[2:4, 0:16] = (index_v[0] + h * NC).astype(F32)
    lane = iota((8, NV), 1)
    half_lo = jnp.where(lane == 0, 0.0, 0.5).astype(F32)
    half_hi = jnp.where(lane == NV - 1, 0.0, 0.5).astype(F32)
    on = [jnp.where((h * 4 + q >= 0) & (h * 4 + q < planes[0]), 1.0 / 64, 0.0) for q in range(-3, 7)]

    def place(q):
        if q < 0:
            return from_left, q + 3
        if q < 3:
            return left, q
        if q == 3:
            return right, 2
        return from_right, q - 4

    for q in range(-3, 7):
        ref, p = place(q)
        for c in range(4):
            row = 12 * NV + 4 * p + c
            rho_s[q + 3, c] = jnp.broadcast_to(ref[row : row + 1, :], (8, NV))

    def smooth_third(x):
        return x + half_lo * pltpu.roll(x, 1, 1) + half_hi * pltpu.roll(x, NV - 1, 1)

    def apply(cells, lo):
        dense = [[rho_s[lo + i, c] * x for c, x in enumerate(row)] for i, row in enumerate(cells)]
        plain, dense = smooth_first(cells), smooth_first(dense)
        out = []
        for i, (pr, dr) in enumerate(zip(plain, dense)):
            pr, dr = smooth_second(pr), smooth_second(dr)
            q = lo + 1 + i
            out.append(
                [(rho_s[q, c] * smooth_third(x) + smooth_third(y)) * on[q] for c, (x, y) in enumerate(zip(pr, dr))]
            )
        return out

    def group(g, carry):
        cells = []
        for q in range(-3, 7):
            ref, p = place(q)
            cells.append([ref[pl.ds(pl.multiple_of((4 * p + c) * NV + g * 8, 8), 8), :] for c in range(4)])
        cells = apply(apply(cells, 0), 1)
        rows = pl.ds(pl.multiple_of(32 + g * 8, 8), 8)
        for p in range(4):
            for c in range(4):
                k = 4 * p + c
                both[rows, k * NV : (k + 1) * NV] = cells[p + 1][c]
        cells = apply(cells, 2)
        rows = pl.ds(pl.multiple_of(32 + NV + g * 8, 8), 8)
        for p in range(4):
            for c in range(4):
                k = 4 * p + c
                both[rows, k * NV : (k + 1) * NV] = cells[p][c]
        return carry

    lax.fori_loop(0, NV // 8, group, 0, unroll=2)
    fill_hot(index, both, F32)
    w_out[...] = both[32 : 32 + NV, :]
    gram = dot_nt(both[: 32 + NV, :], both[32:, :])
    wg_out[...] = gram[:32, :NV]
    row, col = iota((NV, NV), 0), iota((NV, NV), 1)
    s, c = gram[32:, :NV], gram[32:, NV:]
    packed = jnp.where(row >= col, s, c)
    diag = jnp.sum(jnp.where(row == col, c, 0.0), axis=0, keepdims=True)
    for peer in range(8):
        full_out[peer, :NV, :] = packed
        full_out[peer, NV:, :] = jnp.broadcast_to(diag, (8, NV))


def fill_hot(index, hot, dtype):
    for part in range(4):
        sub = iota((8, NV), 0)
        col = jnp.zeros((8, NV), jnp.int32)
        for j in range(8):
            col = jnp.where(sub == j, index[0, part // 2, (part % 2) * 8 + j], col)
        lane = iota((8, NV), 1)
        for k in range(16):
            hot[part * 8 : part * 8 + 8, k * NV : (k + 1) * NV] = jnp.where(col == lane + k * NV, 1.0, 0.0).astype(dtype)


def own_kernel(full, wg, small, li_out, k_out, message):
    h = lax.axis_index("halo")
    total = jnp.sum(full[...], axis=0)
    packed, diag = total[:NV, :], total[NV : NV + 1, :]
    row, col = iota((NV, NV), 0), iota((NV, NV), 1)
    mirror = packed.T
    s = jnp.where(row >= col, packed, mirror)
    c = jnp.where(row < col, packed, jnp.where(row > col, mirror, diag))
    (li,) = chol_inv([s])
    k = dot_nt(dot_nn(li, c), li)
    li_out[...] = li
    k_out[...] = k
    rows = dot_nt(wg[...], li)
    lane, sub = iota((8, NV), 1), iota((8, NV), 0)
    tile = small[...]
    tile = jnp.where(sub < 4, tile, pltpu.roll(pltpu.roll(tile, NV - 8, 1), 4, 0))
    tile = pltpu.roll(tile, h * 16, 1)
    upper = k_out[pl.ds(pl.multiple_of(h * 16, 16), 8), :]
    lower = k_out[pl.ds(pl.multiple_of(h * 16 + 8, 8), 8), :]
    lower = jnp.where((lane >= h * 16) & (lane < h * 16 + 8), tile, lower)
    for peer in range(SQ):
        message[peer, :8, :] = upper
        message[peer, 8:16, :] = lower
        message[peer, 16:, :] = rows


def invert(order, inverse):
    for t in range(SQ * SQ):
        inverse[order[t]] = t


def select_kernel(order, got, out, inverse):
    odd = lax.axis_index("halo") % 2 == 1
    leaf = lax.axis_index("leaf")
    y, z = leaf // SQ, leaf % SQ
    invert(order, inverse)
    for to in range(SQ):
        position = order[jnp.where(odd, y * SQ + to, to * SQ + z)]
        for role in range(1, 4):
            source = inverse[position ^ role]
            row, col = source // SQ, source % SQ

            @pl.when(jnp.where(odd, col == z, row == y))
            def _(to=to, role=role, at=jnp.where(odd, row, col)):
                out[to, (role - 1) * ROWS : role * ROWS, :] = got[at]


def collect_kernel(order, got, message, out, inverse):
    odd = lax.axis_index("halo") % 2 == 1
    leaf = lax.axis_index("leaf")
    invert(order, inverse)
    position = order[leaf]
    parts = []
    for r in range(1, 4):
        source = inverse[position ^ r]
        parts.append(got[jnp.where(odd, source % SQ, source // SQ), (r - 1) * ROWS : r * ROWS, :])
    own = message[0, 8:, :]
    for peer in range(4):
        for r in range(3):
            out[peer, r * ROWS : (r + 1) * ROWS, :] = parts[r]
        out[peer, 3 * ROWS :, :] = own


def solve_kernel(
    order, index, mine, other, k_own, li, w, start, modes_out, reduced_out, inverse, kmat, rmat, big, z_s, hot
):
    h, leaf = lax.axis_index("halo"), lax.axis_index("leaf")
    odd = h % 2
    invert(order, inverse)
    position = order[leaf]
    ids = [leaf] + [inverse[position ^ role] for role in range(1, 4)]
    scale = 0.5 * math.sqrt(NC * 8 / NV)

    def piece(halo, lo, hi):
        a, b = mine[halo // 2, lo:hi, :], other[halo // 2, lo:hi, :]
        return jnp.where(odd == halo % 2, a, b)

    row, col = iota((NV, NV), 0), iota((NV, NV), 1)
    eye = row == col
    lane = iota((8, NV), 1)
    small = []
    kmat[0] = k_own[...]
    for role in range(4):
        base = 3 * ROWS - 8 if role == 0 else (role - 1) * ROWS
        tile = jnp.zeros((8, NV), F32)
        for halo in range(8):
            at = slice(16 * halo, 16 * halo + 16)
            lower = piece(halo, base + 8, base + 16)
            if role:
                kmat[role, 16 * halo : 16 * halo + 8, :] = piece(halo, base, base + 8)
                kmat[role, 16 * halo + 8 : 16 * halo + 16, :] = lower
            rmat[0, role, at, :] = piece(halo, base + 16, base + 32)
            rmat[1, role, at, :] = piece(halo, base + 32, base + 48)
            tile = jnp.where((lane >= 16 * halo) & (lane < 16 * halo + 8), lower, tile)
        small.append(tile + pltpu.roll(pltpu.roll(tile, 8, 1), 4, 0))
        if role:
            raw = kmat[role]
            kmat[role] = jnp.where(row <= col, raw, raw.T)

    def meet(slot, first, ka, ra, kb, rb, stiff):
        ra, rb = scale * ra, scale * rb
        r1, r2 = jnp.where(first, ra, rb), jnp.where(first, rb, ra)
        big[slot, :NV, :NV] = jnp.where(first, ka, kb)
        big[slot, :NV, NV:] = r1.T
        big[slot, NV : 2 * NV, :NV] = jnp.where(first, kb, ka)
        big[slot, NV : 2 * NV, NV:] = r2.T
        big[slot, 2 * NV :, :NV] = r1
        big[slot, 2 * NV :, NV:] = r2
        return jnp.sum(jnp.where(eye, stiff, 0.0), axis=1, keepdims=True)

    def product(slot, diag, x):
        x1, x2, x3 = x[:NV], x[NV : 2 * NV], x[2 * NV :]
        y1 = dot_nn(big[slot, :NV], jnp.concatenate([x1, x3], axis=0))
        y2 = dot_nn(big[slot, NV : 2 * NV], jnp.concatenate([x2, x3], axis=0))
        y3 = dot_nn(big[slot, 2 * NV :], x[: 2 * NV]) + diag * x3
        return jnp.concatenate([y1, y2, y3], axis=0)

    def reduce(diags):
        ys = [product(i, d, start[...]) for i, d in enumerate(diags)]
        ys = [product(i, d, y) for i, (d, y) in enumerate(zip(diags, ys))]
        ps = chol_inv([dot_tn(y, y) for y in ys])
        images = [dot_tn(y, product(i, d, y)) for i, (d, y) in enumerate(zip(diags, ys))]
        return [dot_nt(y, p) for y, p in zip(ys, ps)], [dot_nt(dot_nn(p, im), p) for p, im in zip(ps, images)]

    firsts = [ids[0] < ids[1], ids[2] < ids[3]]
    diags = []
    for pair in range(2):
        a, b = 2 * pair, 2 * pair + 1
        diag = meet(pair, firsts[pair], kmat[a], rmat[0, a], kmat[b], rmat[0, b], small[a][0:1] + small[b][0:1])
        diags.append(diag)
    zs, ks = reduce(diags)
    joint = []
    for pair in range(2):
        z = zs[pair]
        lo, hi, zi = z[:NV], z[NV : 2 * NV], z[2 * NV :]
        za, zb = jnp.where(firsts[pair], lo, hi), jnp.where(firsts[pair], hi, lo)
        match = jnp.zeros((NV, NV), F32)
        for role in (2 * pair, 2 * pair + 1):
            up = jnp.sum(jnp.where(eye, small[role][3:4], 0.0), axis=1, keepdims=True)
            match = match + jnp.where(up == small[role][2:3], 1.0, 0.0)
        joint.append(
            dot_nn(rmat[1, 2 * pair], za) + dot_nn(rmat[1, 2 * pair + 1], zb) + math.sqrt(0.5) * dot_nn(match, zi)
        )
        if pair == 0:
            z_s[:NV, :] = za
            z_s[NV:, :] = zi
    first = jnp.minimum(ids[0], ids[1]) < jnp.minimum(ids[2], ids[3])
    stiff = small[0][1:2] + small[1][1:2] + small[2][1:2] + small[3][1:2]
    diag = meet(0, first, ks[0], joint[0], ks[1], joint[1], stiff)
    (z1,), (k1,) = reduce([diag])
    reduced_out[...] = k1
    top = jnp.where(first, z1[:NV], z1[NV : 2 * NV])
    at = pl.ds(pl.multiple_of(NV + h * 16, 16), 16)
    low_part = z_s[at, :]
    z_low = z_s[:NV, :]
    z_s[NV:, :] = z1[2 * NV :]
    top_part = z_s[at, :]
    final = math.sqrt(NC * 8)
    mixed = final * dot_tn(top, dot_tn(z_low, li[...]))
    spread = jnp.concatenate([math.sqrt(0.5) * final * dot_nn(low_part, top), 0.5 * final * top_part], axis=0)
    fill_hot(index, hot, BF)
    l_hi, l_lo = split(jnp.concatenate([mixed, spread.T], axis=1))
    for k in range(0, 16, 2):
        at = slice(k * NV, (k + 2) * NV)
        r_hi, r_lo = split(w[:, at])
        tail = jnp.concatenate([r_hi, hot[:, at]], axis=0)
        part = dot_bf(l_lo, tail) + dot_bf(l_hi[:, :NV], r_lo) + dot_bf(l_hi, tail)
        modes_out[pl.ds(k, NV, stride=16), :] = part[:, :NV]
        modes_out[pl.ds(k + 1, NV, stride=16), :] = part[:, NV:]


def per_device(start_modes, density, planes, tree_order, iface_index, iface_stiff, reduced_start):
    rows = [[h * 64 + y * SQ + z for z in range(SQ)] for h in range(8) for y in range(SQ)]
    cols = [[h * 64 + y * SQ + z for y in range(SQ)] for h in range(8) for z in range(SQ)]
    even = [h % 2 == 0 for h in range(8) for _ in range(SQ)]
    first_groups = [r if e else c for e, r, c in zip(even, rows, cols)]
    second_groups = [c if e else r for e, r, c in zip(even, rows, cols)]
    everyone = ("halo", "leaf")
    chips = [[0, 2, 4, 6], [1, 3, 5, 7]]
    edge = 12 * NV + 16
    left, right = pl.pallas_call(
        prep_kernel,
        out_shape=(shape(edge, NV), shape(edge, NV)),
        in_specs=[SM, FAR, FAR],
        out_specs=(VM, VM),
        scratch_shapes=[
            pltpu.VMEM((NC, NV), BF),
            pltpu.VMEM((NC, NV), F32),
            pltpu.VMEM((16, NV), F32),
            pltpu.SemaphoreType.DMA((5,)),
        ],
        name="prep",
        compiler_params=grant(8),
    )(planes, far(start_modes.reshape(NC, NV)), far(density.reshape(16, NV)))
    from_left = lax.ppermute(right, "halo", [(i, i + 1) for i in range(7)])
    from_right = lax.ppermute(left, "halo", [(i + 1, i) for i in range(7)])
    w, full, wg, small = pl.pallas_call(
        front_kernel,
        out_shape=(shape(NV, NC), shape(8, NV + 8, NV), shape(32, NV), shape(8, NV)),
        in_specs=[SM, SM, VM, VM, VM, VM, VM, VM],
        out_specs=(VM, VM, VM, VM),
        scratch_shapes=[
            pltpu.VMEM((10, 4, 8, NV), F32),
            pltpu.VMEM((32 + 2 * NV, NC), F32),
        ],
        name="front",
        compiler_params=grant(24),
    )(planes, iface_index, iface_stiff, iface_index, left, right, from_left, from_right)
    full = lax.all_to_all(full, "halo", 0, 0, tiled=True)
    li, k_own, message = pl.pallas_call(
        own_kernel,
        out_shape=(shape(NV, NV), shape(NV, NV), shape(SQ, ROWS, NV)),
        in_specs=[VM, VM, VM],
        out_specs=(VM, VM, VM),
        name="own",
        compiler_params=grant(8),
    )(full, wg, small)
    along = lax.all_to_all(message, everyone, 0, 0, tiled=True, axis_index_groups=first_groups)
    chosen = pl.pallas_call(
        select_kernel,
        out_shape=shape(SQ, 3 * ROWS, NV),
        in_specs=[SM, VM],
        out_specs=VM,
        scratch_shapes=[pltpu.SMEM((SQ * SQ,), jnp.int32)],
        name="select",
        compiler_params=grant(4),
    )(tree_order, along)
    across = lax.all_to_all(chosen, everyone, 0, 0, tiled=True, axis_index_groups=second_groups)
    gathered = pl.pallas_call(
        collect_kernel,
        out_shape=shape(4, AG, NV),
        in_specs=[SM, VM, VM],
        out_specs=VM,
        scratch_shapes=[pltpu.SMEM((SQ * SQ,), jnp.int32)],
        name="collect",
        compiler_params=grant(4),
    )(tree_order, across, message)
    mine = lax.all_to_all(gathered, "halo", 0, 0, tiled=True, axis_index_groups=chips)
    other = lax.ppermute(mine, "halo", [(i, i ^ 1) for i in range(8)])
    modes, reduced = pl.pallas_call(
        solve_kernel,
        out_shape=(shape(NC, NV), shape(NV, NV)),
        in_specs=[SM, SM, VM, VM, VM, VM, VM, VM],
        out_specs=(VM, VM),
        scratch_shapes=[
            pltpu.SMEM((SQ * SQ,), jnp.int32),
            pltpu.VMEM((4, NV, NV), F32),
            pltpu.VMEM((2, 4, NV, NV), F32),
            pltpu.VMEM((2, 3 * NV, 2 * NV), F32),
            pltpu.VMEM((2 * NV, NV), F32),
            pltpu.VMEM((32, NC), BF),
        ],
        name="solve",
        compiler_params=grant(20),
    )(tree_order, iface_index, mine, other, k_own, li, w, reduced_start)
    return modes.reshape(1, NV, 4, 4, NV), reduced[None]


def solution(mesh):
    return jax.shard_map(
        per_device,
        mesh=mesh,
        in_specs=(
            P("leaf", None, "halo", None, None),
            P("leaf", "halo", None, None),
            P("leaf"),
            P(),
            P("leaf", None, "halo"),
            P("leaf", None, "halo"),
            P(),
        ),
        out_specs=(P("leaf", None, "halo", None, None), P("leaf", None, None)),
        check_vma=False,
    )
```

```python
import math

import jax
import jax.numpy as jnp
from jax import lax
from jax.experimental import pallas as pl
from jax.experimental.pallas import tpu as pltpu
from jax.sharding import PartitionSpec as P

F32, BF = jnp.float32, jnp.bfloat16
HI = lax.Precision.HIGHEST
NV = 128
NC = 2048
SQ = 8
ROWS = 48
AG = 3 * ROWS + 40
VM = pl.BlockSpec(memory_space=pltpu.VMEM)
SM = pl.BlockSpec(memory_space=pltpu.SMEM)
FAR = pl.BlockSpec(memory_space=pltpu.HBM)


def dot_nt(a, b):
    return lax.dot_general(a, b, (((1,), (1,)), ((), ())), precision=HI, preferred_element_type=F32)


def dot_nn(a, b):
    return lax.dot_general(a, b, (((1,), (0,)), ((), ())), precision=HI, preferred_element_type=F32)


def dot_tn(a, b):
    return lax.dot_general(a, b, (((0,), (0,)), ((), ())), precision=HI, preferred_element_type=F32)


def dot_bf(a, b):
    return lax.dot_general(a, b, (((1,), (0,)), ((), ())), preferred_element_type=F32)


def split(x):
    hi = x.astype(BF)
    return hi, (x - hi.astype(F32)).astype(BF)


def iota(shape, dim):
    return lax.broadcasted_iota(jnp.int32, shape, dim)


def far(x):
    return pltpu.with_memory_space_constraint(x, pltpu.HBM)


def grant(mib):
    return pltpu.CompilerParams(vmem_limit_bytes=mib << 20)


def shape(*dims):
    return jax.ShapeDtypeStruct(dims, F32)


def eliminate(mats):
    side = len(mats)
    width = NV // side
    n = width // 8
    sh = (8, NV)
    lane, sub = iota(sh, 1), iota(sh, 0)
    base = lane - lane % width
    lane = lane - base

    def over_lanes(x, c):
        if side == 1:
            return jnp.broadcast_to(x[:, c : c + 1], sh)
        return jnp.take_along_axis(x, base + c, axis=1)

    def over_subs(x, r):
        return jnp.broadcast_to(x[r : r + 1, :], sh)

    whole = jnp.concatenate(mats, axis=1) if side > 1 else mats[0]
    rows = [whole[8 * i : 8 * i + 8, :] for i in range(n)]
    ready = [over_lanes(rows[0], j) for j in range(8)]
    for s in range(n):
        p, cols = rows[s], ready
        inside = (lane >= 8 * s) & (lane < 8 * s + 8)
        after = s + 1 < n
        if after:
            q = rows[s + 1]
            mine = [over_lanes(q, 8 * s + j) for j in range(8)]
            ready = [over_lanes(q, 8 * s + 8 + j) for j in range(8)]
            q = jnp.where(inside, 0.0, q)
        scaled, kept, scales, upper = [], [], [], {}
        for k in range(8):
            rs = lax.rsqrt(over_subs(cols[k], k))
            at = lane == 8 * s + k
            r = jnp.where(at, rs, over_subs(p, k) * rs)
            scaled.append(r)
            scales.append(rs)
            kept.append(jnp.where(inside & (lane > 8 * s + k), 0.0, r))
            if k < 7:
                low = cols[k] * rs
                for j in range(k + 1, 8):
                    upper[k, j] = over_subs(cols[j], k) * rs
                    cols[j] = cols[j] - low * upper[k, j]
                p = jnp.where(sub > k, jnp.where(at, 0.0, p) - low * r, p)
            if after:
                low = mine[k] * rs
                for j in range(k + 1, 8):
                    mine[j] = mine[j] - low * upper[k, j]
                for j in range(8):
                    ready[j] = ready[j] - low * over_subs(low, j)
                q = q - low * kept[k]
        out = scaled[7]
        for k in range(7):
            out = jnp.where(sub == k, scaled[k], out)
        rows[s] = jnp.where(lane > 8 * s + sub, 0.0, out)
        if after:
            rows[s + 1] = q
        for a in range(s + 2, n):
            q = rows[a]
            cols = [over_lanes(q, 8 * s + j) for j in range(8)]
            q = jnp.where(inside, 0.0, q)
            for k in range(8):
                low = cols[k] * scales[k]
                q = q - low * kept[k]
                for j in range(k + 1, 8):
                    cols[j] = cols[j] - low * upper[k, j]
            rows[a] = q
    whole = jnp.concatenate(rows, axis=0)
    return [whole[:, width * b : width * (b + 1)] for b in range(side)]


def chol_inv(mats):
    if len(mats) == 1:
        return eliminate(mats)
    half = NV // 2
    tops = eliminate([m[:half, :half] for m in mats])
    sides = [dot_nt(m[half:, :half], t) for m, t in zip(mats, tops)]
    ends = eliminate([m[half:, half:] - dot_nt(x, x) for m, x in zip(mats, sides)])
    lows = [dot_nn(e, dot_nn(x, t)) for x, t, e in zip(sides, tops, ends)]
    zero = jnp.zeros((half, half), F32)
    return [
        jnp.concatenate([jnp.concatenate([t, zero], axis=1), jnp.concatenate([-x, e], axis=1)], axis=0)
        for t, x, e in zip(tops, lows, ends)
    ]


def prep_kernel(planes, v_far, rho_far, chip, link, v, wide, rho, sems):
    h = lax.axis_index("halo")
    odd = h % 2 == 1
    step = NC // 4
    copies = [
        pltpu.make_async_copy(v_far.at[i * step : (i + 1) * step], v.at[i * step : (i + 1) * step], sems.at[i])
        for i in range(4)
    ]
    copies.append(pltpu.make_async_copy(rho_far, rho, sems.at[4]))
    for copy in copies:
        copy.start()
    for i in range(4):
        copies[i].wait()
        wide[i * step : (i + 1) * step, :] = v[i * step : (i + 1) * step, :].astype(F32)
        parts = []
        for k in range(16):
            part = wide[pl.ds(i * step + k, NV // 4, stride=16), :]
            parts.append(jnp.where(h * 4 + k // 4 < planes[0], part, 0.0))
        for k in range(12):
            at = slice(k * NV + i * (NV // 4), k * NV + (i + 1) * (NV // 4))
            chip[at, :] = jnp.where(odd, parts[k], parts[k + 4])
            link[at, :] = jnp.where(odd, parts[k + 4], parts[k])
    copies[4].wait()
    lo, hi = rho[...], jnp.concatenate([rho[4:, :], rho[:4, :]], axis=0)
    chip[12 * NV :, :] = jnp.where(odd, lo, hi)
    link[12 * NV :, :] = jnp.where(odd, hi, lo)


def smooth_first(cells):
    pairs = [[a + b for a, b in zip(lo, hi)] for lo, hi in zip(cells[:-1], cells[1:])]
    return [[a + b for a, b in zip(lo, hi)] for lo, hi in zip(pairs[:-1], pairs[1:])]


def smooth_second(row):
    pairs = [a + b for a, b in zip(row[:-1], row[1:])]
    return [a + b for a, b in zip([row[0]] + pairs, pairs + [row[-1]])]


def front_kernel(
    planes, index, stiff, index_v, chip, link, from_chip, from_link, w_out, full_out, wg_out, tile_out, rho_s, both
):
    h = lax.axis_index("halo")
    tile_out[...] = jnp.zeros((8, NV), F32)
    tile_out[0:2, 0:16] = stiff[0]
    tile_out[2:4, 0:16] = (index_v[0] + h * NC).astype(F32)
    lane = iota((8, NV), 1)
    half_lo = jnp.where(lane == 0, 0.0, 0.5).astype(F32)
    half_hi = jnp.where(lane == NV - 1, 0.0, 0.5).astype(F32)
    on = [jnp.where((h * 4 + q >= 0) & (h * 4 + q < planes[0]), 1.0 / 64, 0.0) for q in range(-3, 7)]

    odd = h % 2 == 1

    def place(q):
        if q < 0:
            return (from_link, q + 3), (from_chip, q + 3)
        if q < 3:
            return (link, q), (chip, q)
        if q == 3:
            return (chip, 2), (link, 2)
        return (from_chip, q - 4), (from_link, q - 4)

    for q in range(-3, 7):
        (even_ref, p), (odd_ref, _) = place(q)
        for c in range(4):
            at = slice(12 * NV + 4 * p + c, 12 * NV + 4 * p + c + 1)
            rho_s[q + 3, c] = jnp.broadcast_to(jnp.where(odd, odd_ref[at, :], even_ref[at, :]), (8, NV))

    def smooth_third(x):
        return x + half_lo * pltpu.roll(x, 1, 1) + half_hi * pltpu.roll(x, NV - 1, 1)

    def apply(cells, lo):
        dense = [[rho_s[lo + i, c] * x for c, x in enumerate(row)] for i, row in enumerate(cells)]
        plain, dense = smooth_first(cells), smooth_first(dense)
        out = []
        for i, (pr, dr) in enumerate(zip(plain, dense)):
            pr, dr = smooth_second(pr), smooth_second(dr)
            q = lo + 1 + i
            out.append(
                [(rho_s[q, c] * smooth_third(x) + smooth_third(y)) * on[q] for c, (x, y) in enumerate(zip(pr, dr))]
            )
        return out

    def group(g, carry):
        cells = []
        for q in range(-3, 7):
            (even_ref, p), (odd_ref, _) = place(q)
            at = [pl.ds(pl.multiple_of((4 * p + c) * NV + g * 8, 8), 8) for c in range(4)]
            cells.append([jnp.where(odd, odd_ref[a, :], even_ref[a, :]) for a in at])
        cells = apply(apply(cells, 0), 1)
        rows = pl.ds(pl.multiple_of(32 + g * 8, 8), 8)
        for p in range(4):
            for c in range(4):
                k = 4 * p + c
                both[rows, k * NV : (k + 1) * NV] = cells[p + 1][c]
        cells = apply(cells, 2)
        rows = pl.ds(pl.multiple_of(32 + NV + g * 8, 8), 8)
        for p in range(4):
            for c in range(4):
                k = 4 * p + c
                both[rows, k * NV : (k + 1) * NV] = cells[p][c]
        return carry

    lax.fori_loop(0, NV // 8, group, 0, unroll=2)
    fill_hot(index, both, F32)
    w_out[...] = both[32 : 32 + NV, :]
    gram = dot_nt(both[: 32 + NV, :], both[32:, :])
    wg_out[...] = gram[:32, :NV]
    row, col = iota((NV, NV), 0), iota((NV, NV), 1)
    s, c = gram[32:, :NV], gram[32:, NV:]
    packed = jnp.where(row >= col, s, c)
    diag = jnp.sum(jnp.where(row == col, c, 0.0), axis=0, keepdims=True)
    for peer in range(8):
        full_out[peer, :NV, :] = packed
        full_out[peer, NV:, :] = jnp.broadcast_to(diag, (8, NV))


def fill_hot(index, hot, dtype):
    for part in range(4):
        sub = iota((8, NV), 0)
        col = jnp.zeros((8, NV), jnp.int32)
        for j in range(8):
            col = jnp.where(sub == j, index[0, part // 2, (part % 2) * 8 + j], col)
        lane = iota((8, NV), 1)
        for k in range(16):
            hot[part * 8 : part * 8 + 8, k * NV : (k + 1) * NV] = jnp.where(col == lane + k * NV, 1.0, 0.0).astype(dtype)


def own_kernel(full, wg, small, li_out, k_out, message):
    h = lax.axis_index("halo")
    total = jnp.sum(full[...], axis=0)
    packed, diag = total[:NV, :], total[NV : NV + 1, :]
    row, col = iota((NV, NV), 0), iota((NV, NV), 1)
    mirror = packed.T
    s = jnp.where(row >= col, packed, mirror)
    c = jnp.where(row < col, packed, jnp.where(row > col, mirror, diag))
    (li,) = chol_inv([s])
    k = dot_nt(dot_nn(li, c), li)
    li_out[...] = li
    k_out[...] = k
    rows = dot_nt(wg[...], li)
    lane, sub = iota((8, NV), 1), iota((8, NV), 0)
    tile = small[...]
    tile = jnp.where(sub < 4, tile, pltpu.roll(pltpu.roll(tile, NV - 8, 1), 4, 0))
    tile = pltpu.roll(tile, h * 16, 1)
    upper = k_out[pl.ds(pl.multiple_of(h * 16, 16), 8), :]
    lower = k_out[pl.ds(pl.multiple_of(h * 16 + 8, 8), 8), :]
    lower = jnp.where((lane >= h * 16) & (lane < h * 16 + 8), tile, lower)
    for peer in range(SQ):
        message[peer, :8, :] = upper
        message[peer, 8:16, :] = lower
        message[peer, 16:, :] = rows


def invert(order, inverse):
    for t in range(SQ * SQ):
        inverse[order[t]] = t


def select_kernel(order, got, out, inverse):
    odd = lax.axis_index("halo") % 2 == 1
    leaf = lax.axis_index("leaf")
    y, z = leaf // SQ, leaf % SQ
    invert(order, inverse)
    for to in range(SQ):
        position = order[jnp.where(odd, y * SQ + to, to * SQ + z)]
        for role in range(1, 4):
            source = inverse[position ^ role]
            row, col = source // SQ, source % SQ

            @pl.when(jnp.where(odd, col == z, row == y))
            def _(to=to, role=role, at=jnp.where(odd, row, col)):
                out[to, (role - 1) * ROWS : role * ROWS, :] = got[at]


def collect_kernel(order, got, message, out, inverse):
    odd = lax.axis_index("halo") % 2 == 1
    leaf = lax.axis_index("leaf")
    invert(order, inverse)
    position = order[leaf]
    parts = []
    for r in range(1, 4):
        source = inverse[position ^ r]
        parts.append(got[jnp.where(odd, source % SQ, source // SQ), (r - 1) * ROWS : r * ROWS, :])
    own = message[0, 8:, :]
    for peer in range(4):
        for r in range(3):
            out[peer, r * ROWS : (r + 1) * ROWS, :] = parts[r]
        out[peer, 3 * ROWS :, :] = own


def solve_kernel(
    order, index, mine, other, k_own, li, w, start, modes_out, reduced_out, inverse, kmat, rmat, big, z_s, hot
):
    h, leaf = lax.axis_index("halo"), lax.axis_index("leaf")
    odd = h % 2
    invert(order, inverse)
    position = order[leaf]
    ids = [leaf] + [inverse[position ^ role] for role in range(1, 4)]
    scale = 0.5 * math.sqrt(NC * 8 / NV)

    def piece(halo, lo, hi):
        a, b = mine[halo // 2, lo:hi, :], other[halo // 2, lo:hi, :]
        return jnp.where(odd == halo % 2, a, b)

    row, col = iota((NV, NV), 0), iota((NV, NV), 1)
    eye = row == col
    lane = iota((8, NV), 1)
    small = []
    kmat[0] = k_own[...]
    for role in range(4):
        base = 3 * ROWS - 8 if role == 0 else (role - 1) * ROWS
        tile = jnp.zeros((8, NV), F32)
        for halo in range(8):
            at = slice(16 * halo, 16 * halo + 16)
            lower = piece(halo, base + 8, base + 16)
            if role:
                kmat[role, 16 * halo : 16 * halo + 8, :] = piece(halo, base, base + 8)
                kmat[role, 16 * halo + 8 : 16 * halo + 16, :] = lower
            rmat[0, role, at, :] = piece(halo, base + 16, base + 32)
            rmat[1, role, at, :] = piece(halo, base + 32, base + 48)
            tile = jnp.where((lane >= 16 * halo) & (lane < 16 * halo + 8), lower, tile)
        small.append(tile + pltpu.roll(pltpu.roll(tile, 8, 1), 4, 0))
        if role:
            raw = kmat[role]
            kmat[role] = jnp.where(row <= col, raw, raw.T)

    def meet(slot, first, ka, ra, kb, rb, stiff):
        ra, rb = scale * ra, scale * rb
        r1, r2 = jnp.where(first, ra, rb), jnp.where(first, rb, ra)
        big[slot, :NV, :NV] = jnp.where(first, ka, kb)
        big[slot, :NV, NV:] = r1.T
        big[slot, NV : 2 * NV, :NV] = jnp.where(first, kb, ka)
        big[slot, NV : 2 * NV, NV:] = r2.T
        big[slot, 2 * NV :, :NV] = r1
        big[slot, 2 * NV :, NV:] = r2
        return jnp.sum(jnp.where(eye, stiff, 0.0), axis=1, keepdims=True)

    def product(slot, diag, x):
        x1, x2, x3 = x[:NV], x[NV : 2 * NV], x[2 * NV :]
        y1 = dot_nn(big[slot, :NV], jnp.concatenate([x1, x3], axis=0))
        y2 = dot_nn(big[slot, NV : 2 * NV], jnp.concatenate([x2, x3], axis=0))
        y3 = dot_nn(big[slot, 2 * NV :], x[: 2 * NV]) + diag * x3
        return jnp.concatenate([y1, y2, y3], axis=0)

    def reduce(diags):
        ys = [product(i, d, start[...]) for i, d in enumerate(diags)]
        ys = [product(i, d, y) for i, (d, y) in enumerate(zip(diags, ys))]
        ps = chol_inv([dot_tn(y, y) for y in ys])
        images = [dot_tn(y, product(i, d, y)) for i, (d, y) in enumerate(zip(diags, ys))]
        return [dot_nt(y, p) for y, p in zip(ys, ps)], [dot_nt(dot_nn(p, im), p) for p, im in zip(ps, images)]

    firsts = [ids[0] < ids[1], ids[2] < ids[3]]
    diags = []
    for pair in range(2):
        a, b = 2 * pair, 2 * pair + 1
        diag = meet(pair, firsts[pair], kmat[a], rmat[0, a], kmat[b], rmat[0, b], small[a][0:1] + small[b][0:1])
        diags.append(diag)
    zs, ks = reduce(diags)
    joint = []
    for pair in range(2):
        z = zs[pair]
        lo, hi, zi = z[:NV], z[NV : 2 * NV], z[2 * NV :]
        za, zb = jnp.where(firsts[pair], lo, hi), jnp.where(firsts[pair], hi, lo)
        match = jnp.zeros((NV, NV), F32)
        for role in (2 * pair, 2 * pair + 1):
            up = jnp.sum(jnp.where(eye, small[role][3:4], 0.0), axis=1, keepdims=True)
            match = match + jnp.where(up == small[role][2:3], 1.0, 0.0)
        joint.append(
            dot_nn(rmat[1, 2 * pair], za) + dot_nn(rmat[1, 2 * pair + 1], zb) + math.sqrt(0.5) * dot_nn(match, zi)
        )
        if pair == 0:
            z_s[:NV, :] = za
            z_s[NV:, :] = zi
    first = jnp.minimum(ids[0], ids[1]) < jnp.minimum(ids[2], ids[3])
    stiff = small[0][1:2] + small[1][1:2] + small[2][1:2] + small[3][1:2]
    diag = meet(0, first, ks[0], joint[0], ks[1], joint[1], stiff)
    (z1,), (k1,) = reduce([diag])
    reduced_out[...] = k1
    top = jnp.where(first, z1[:NV], z1[NV : 2 * NV])
    at = pl.ds(pl.multiple_of(NV + h * 16, 16), 16)
    low_part = z_s[at, :]
    z_low = z_s[:NV, :]
    z_s[NV:, :] = z1[2 * NV :]
    top_part = z_s[at, :]
    final = math.sqrt(NC * 8)
    mixed = final * dot_tn(top, dot_tn(z_low, li[...]))
    spread = jnp.concatenate([math.sqrt(0.5) * final * dot_nn(low_part, top), 0.5 * final * top_part], axis=0)
    fill_hot(index, hot, BF)
    l_hi, l_lo = split(jnp.concatenate([mixed, spread.T], axis=1))
    for k in range(0, 16, 2):
        at = slice(k * NV, (k + 2) * NV)
        r_hi, r_lo = split(w[:, at])
        tail = jnp.concatenate([r_hi, hot[:, at]], axis=0)
        part = dot_bf(l_lo, tail) + dot_bf(l_hi[:, :NV], r_lo) + dot_bf(l_hi, tail)
        modes_out[pl.ds(k, NV, stride=16), :] = part[:, :NV]
        modes_out[pl.ds(k + 1, NV, stride=16), :] = part[:, NV:]


def per_device(start_modes, density, planes, tree_order, iface_index, iface_stiff, reduced_start):
    rows = [[h * 64 + y * SQ + z for z in range(SQ)] for h in range(8) for y in range(SQ)]
    cols = [[h * 64 + y * SQ + z for y in range(SQ)] for h in range(8) for z in range(SQ)]
    even = [h % 2 == 0 for h in range(8) for _ in range(SQ)]
    first_groups = [r if e else c for e, r, c in zip(even, rows, cols)]
    second_groups = [c if e else r for e, r, c in zip(even, rows, cols)]
    everyone = ("halo", "leaf")
    chips = [[0, 2, 4, 6], [1, 3, 5, 7]]
    edge = 12 * NV + 16
    chip, link = pl.pallas_call(
        prep_kernel,
        out_shape=(shape(edge, NV), shape(edge, NV)),
        in_specs=[SM, FAR, FAR],
        out_specs=(VM, VM),
        scratch_shapes=[
            pltpu.VMEM((NC, NV), BF),
            pltpu.VMEM((NC, NV), F32),
            pltpu.VMEM((16, NV), F32),
            pltpu.SemaphoreType.DMA((5,)),
        ],
        name="prep",
        compiler_params=grant(8),
    )(planes, far(start_modes.reshape(NC, NV)), far(density.reshape(16, NV)))
    from_link = lax.ppermute(link, "halo", [(i, i + 1 if i % 2 else i - 1) for i in range(1, 7)])
    from_chip = lax.ppermute(chip, "halo", [(i, i ^ 1) for i in range(8)])
    w, full, wg, small = pl.pallas_call(
        front_kernel,
        out_shape=(shape(NV, NC), shape(8, NV + 8, NV), shape(32, NV), shape(8, NV)),
        in_specs=[SM, SM, VM, VM, VM, VM, VM, VM],
        out_specs=(VM, VM, VM, VM),
        scratch_shapes=[
            pltpu.VMEM((10, 4, 8, NV), F32),
            pltpu.VMEM((32 + 2 * NV, NC), F32),
        ],
        name="front",
        compiler_params=grant(24),
    )(planes, iface_index, iface_stiff, iface_index, chip, link, from_chip, from_link)
    full = lax.all_to_all(full, "halo", 0, 0, tiled=True)
    li, k_own, message = pl.pallas_call(
        own_kernel,
        out_shape=(shape(NV, NV), shape(NV, NV), shape(SQ, ROWS, NV)),
        in_specs=[VM, VM, VM],
        out_specs=(VM, VM, VM),
        name="own",
        compiler_params=grant(8),
    )(full, wg, small)
    along = lax.all_to_all(message, everyone, 0, 0, tiled=True, axis_index_groups=first_groups)
    chosen = pl.pallas_call(
        select_kernel,
        out_shape=shape(SQ, 3 * ROWS, NV),
        in_specs=[SM, VM],
        out_specs=VM,
        scratch_shapes=[pltpu.SMEM((SQ * SQ,), jnp.int32)],
        name="select",
        compiler_params=grant(4),
    )(tree_order, along)
    across = lax.all_to_all(chosen, everyone, 0, 0, tiled=True, axis_index_groups=second_groups)
    gathered = pl.pallas_call(
        collect_kernel,
        out_shape=shape(4, AG, NV),
        in_specs=[SM, VM, VM],
        out_specs=VM,
        scratch_shapes=[pltpu.SMEM((SQ * SQ,), jnp.int32)],
        name="collect",
        compiler_params=grant(4),
    )(tree_order, across, message)
    mine = lax.all_to_all(gathered, "halo", 0, 0, tiled=True, axis_index_groups=chips)
    other = lax.ppermute(mine, "halo", [(i, i ^ 1) for i in range(8)])
    modes, reduced = pl.pallas_call(
        solve_kernel,
        out_shape=(shape(NC, NV), shape(NV, NV)),
        in_specs=[SM, SM, VM, VM, VM, VM, VM, VM],
        out_specs=(VM, VM),
        scratch_shapes=[
            pltpu.SMEM((SQ * SQ,), jnp.int32),
            pltpu.VMEM((4, NV, NV), F32),
            pltpu.VMEM((2, 4, NV, NV), F32),
            pltpu.VMEM((2, 3 * NV, 2 * NV), F32),
            pltpu.VMEM((2 * NV, NV), F32),
            pltpu.VMEM((32, NC), BF),
        ],
        name="solve",
        compiler_params=grant(20),
    )(tree_order, iface_index, mine, other, k_own, li, w, reduced_start)
    return modes.reshape(1, NV, 4, 4, NV), reduced[None]


def solution(mesh):
    return jax.shard_map(
        per_device,
        mesh=mesh,
        in_specs=(
            P("leaf", None, "halo", None, None),
            P("leaf", "halo", None, None),
            P("leaf"),
            P(),
            P("leaf", None, "halo"),
            P("leaf", None, "halo"),
            P(),
        ),
        out_specs=(P("leaf", None, "halo", None, None), P("leaf", None, None)),
        check_vma=False,
    )
```
